256 devices in a mesh: dp: 32 (over x, y, core), tensor: 8 (over z).
Axes of the slice: x: 4, y: 4, z: 8, core: 2. Of those that a mesh axis runs over, the one named last changes fastest.
Arguments:
- output_gradient: bfloat16 [8192, 8192], P('dp', 'tensor'), may hold values from -96 to 96
- hidden: bfloat16 [8192, 28672], P('dp', 'tensor'), may hold values from -3 to 3
- adapter_down: bfloat16 [64, 16, 28672], P('dp', None, 'tensor'), may hold values from -0.03125 to 0.03125
- adapter_up: bfloat16 [64, 16, 8192], P('dp', None, 'tensor'), may hold values from -0.0625 to 0.0625
- counts: int32 [64], replicated, may hold values from 32 to 288, as said below
- offsets: int32 [64], replicated, may hold values from 0 to 8160, as said below
- adapter_slot: int32 [64], replicated, may hold values from 0 to 63, as said below
Outputs:
- adapter_hidden_gradient: bfloat16 [8192, 28672], P('dp', 'tensor')
- adapter_down_gradient: float32 [64, 16, 28672], P('dp', None, 'tensor')
- adapter_up_gradient: float32 [64, 16, 8192], P('dp', None, 'tensor')
The draws below stay inside these ranges and needn't reach their ends.
Inputs may be any that keep to these rules, and one draw needn't show every extreme that they name: counts sum to 8192; the last adapter has exactly 32 tokens; exactly one adapter has 288 tokens, every other fewer. Tokens are grouped by adapter in increasing order: offsets[a] is the sum of counts of the adapters before a. `adapter_slot`: every slot holds exactly one adapter; slot k lies on dp index k // 2, and any 64 // 2 adapters in a row lie on distinct dp indices.
All inputs are finite; a program needn't handle non-finite values.
Results may differ from the reference program's by a relative error of at most 0.0075.
Values may be sent and summed in bfloat16 or wider, within the bound.
No kernel may reach another device: no remote copies, remote signals or barrier semaphores. Data moves between devices by JAX's collectives and lax.ppermute only.
A program may use at most 64 MiB of HBM per device.

```python
import math
import jax
import jax.numpy as jnp
import numpy as np
from jax import lax

MODEL_DIM = 8192
HIDDEN_DIM = 28672
ADAPTER_RANK = 16
TOK_DEV = 256
ADP_DEV = 2
MIN_COUNT = 32
MIXTURE_ADAPTERS = 64
TOKENS = 8192


def layout_tables():
    devices = TOKENS // TOK_DEV
    dense_count = TOK_DEV // MIN_COUNT
    long_units = min(4, (devices - 2) // 3)
    drawn_units = devices - 2 - 3 * long_units
    piece_floor = []
    piece_base = []
    piece_head = []
    piece_tail = []
    for long_index in range(long_units):
        piece_floor.append(TOK_DEV - 12)
        piece_base.append(TOK_DEV)
        piece_head.append(long_index)
        piece_tail.append(-1)
        piece_floor.append(TOK_DEV - MIN_COUNT + 4)
        piece_base.append(TOK_DEV)
        piece_head.append(-1)
        piece_tail.append(long_index)
    for drawn_index in range(drawn_units):
        piece_floor.append(TOK_DEV)
        piece_base.append(TOK_DEV)
        piece_head.append(-1)
        piece_tail.append(-1)
    piece_floor.append(TOK_DEV - MIN_COUNT)
    piece_base.append(TOK_DEV - MIN_COUNT)
    piece_head.append(-1)
    piece_tail.append(-1)
    piece_number = len(piece_floor)
    final_piece = piece_number - 1
    needed = MIXTURE_ADAPTERS - dense_count - long_units - 1
    per_piece = [1] * piece_number
    spare_slots = needed - piece_number
    visit_order = list(range(2 * long_units, final_piece)) + list(range(2 * long_units)) + [final_piece]
    moved = True
    while spare_slots > 0 and moved:
        moved = False
        for piece_index in visit_order:
            if spare_slots > 0 and per_piece[piece_index] < piece_floor[piece_index] // MIN_COUNT:
                per_piece[piece_index] += 1
                spare_slots -= 1
                moved = True
    unit_of = []
    within_unit = []
    kind_of = []
    piece_of = []
    rank_of = []
    long_of = []

    def append_row(unit_number, within_number, kind_number, piece_number_row, rank_number, long_number):
        unit_of.append(unit_number)
        within_unit.append(within_number)
        kind_of.append(kind_number)
        piece_of.append(piece_number_row)
        rank_of.append(rank_number)
        long_of.append(long_number)
    for dense_index in range(dense_count):
        append_row(0, dense_index, 0, 0, 0, 0)
    for long_index in range(long_units):
        unit_number = 1 + long_index
        within_number = 0
        for rank_number in range(per_piece[2 * long_index]):
            append_row(unit_number, within_number, 2, 2 * long_index, rank_number, 0)
            within_number += 1
        append_row(unit_number, within_number, 1, 0, 0, long_index)
        within_number += 1
        for rank_number in range(per_piece[2 * long_index + 1]):
            append_row(unit_number, within_number, 2, 2 * long_index + 1, rank_number, 0)
            within_number += 1
    for drawn_index in range(drawn_units):
        unit_number = 1 + long_units + drawn_index
        piece_index = 2 * long_units + drawn_index
        for rank_number in range(per_piece[piece_index]):
            append_row(unit_number, rank_number, 2, piece_index, rank_number, 0)
    unit_number = 1 + long_units + drawn_units
    for rank_number in range(per_piece[final_piece]):
        append_row(unit_number, rank_number, 2, final_piece, rank_number, 0)
    append_row(unit_number, per_piece[final_piece], 0, 0, 0, 0)
    unit_total = unit_number + 1
    return (np.array(unit_of, np.int32), np.array(within_unit, np.int32), np.array(kind_of, np.int32), np.array(piece_of, np.int32), np.array(rank_of, np.int32), np.array(long_of, np.int32), np.array(per_piece, np.int32), np.array(piece_base, np.int32), np.array(piece_head, np.int32), np.array(piece_tail, np.int32), long_units, unit_total)


def split_counts(key):
    tables = layout_tables()
    unit_of, within_unit, kind_of, piece_of, rank_of, long_of = tables[0:6]
    per_piece, piece_base, piece_head, piece_tail, long_units, unit_total = tables[6:12]
    piece_number = piece_base.shape[0]
    base_key = jax.random.fold_in(key, 7)
    big_key, small_key, tail_key, weight_key, shuffle_key = jax.random.split(base_key, 5)
    long_ids = jnp.arange(long_units, dtype=jnp.int32)
    is_big = long_ids == 0
    head_big = jax.random.randint(big_key, (long_units,), 4, 13)
    head_small = jax.random.randint(small_key, (long_units,), 4, 12)
    head_cut = jnp.where(is_big, head_big, head_small)
    tail_low = MIN_COUNT - 12
    tail_span = jnp.maximum(MIN_COUNT - tail_low - head_cut, 1)
    tail_small = tail_low + jax.random.randint(tail_key, (long_units,), 0, tail_span)
    tail_cut = jnp.where(is_big, MIN_COUNT - head_cut, tail_small)
    long_count = TOK_DEV + head_cut + tail_cut
    head_index = jnp.asarray(np.maximum(piece_head, 0))
    tail_index = jnp.asarray(np.maximum(piece_tail, 0))
    head_mask = jnp.asarray(piece_head >= 0)
    tail_mask = jnp.asarray(piece_tail >= 0)
    piece_length = jnp.asarray(piece_base) - jnp.where(head_mask, head_cut[head_index], 0) - jnp.where(tail_mask, tail_cut[tail_index], 0)
    members = ((kind_of == 2)[:, None] & (piece_of[:, None] == np.arange(piece_number)[None, :])).astype(np.int32)
    member_int = jnp.asarray(members)
    filler_mask = jnp.asarray(kind_of == 2)
    piece_ids = jnp.asarray(piece_of)
    weights = jax.random.randint(weight_key, (MIXTURE_ADAPTERS,), 1, 4)
    weight_total = jnp.sum(member_int * weights[:, None], axis=0)
    spare_tokens = piece_length - jnp.asarray(per_piece) * MIN_COUNT
    own_spare = spare_tokens[piece_ids]
    own_total = jnp.maximum(weight_total[piece_ids], 1)
    extras = jnp.where(filler_mask, own_spare * weights // own_total, 0)
    leftover = spare_tokens - jnp.sum(member_int * extras[:, None], axis=0)
    extras = extras + jnp.where(filler_mask & (jnp.asarray(rank_of) < leftover[piece_ids]), 1, 0)
    canonical = jnp.where(jnp.asarray(kind_of == 1), long_count[jnp.asarray(long_of)], jnp.where(filler_mask, MIN_COUNT + extras, MIN_COUNT))
    unit_position = jnp.concatenate([jax.random.permutation(shuffle_key, unit_total - 1).astype(jnp.int32), jnp.array([unit_total - 1], jnp.int32)])
    sort_key = unit_position[jnp.asarray(unit_of)] * MIXTURE_ADAPTERS + jnp.asarray(within_unit)
    ordering = jnp.argsort(sort_key, stable=True)
    return canonical[ordering].astype(jnp.int32)


def draw_counts(key, part):
    return split_counts(key)


def draw_offsets(key, part):
    sizes_drawn = split_counts(key)
    return (jnp.cumsum(sizes_drawn) - sizes_drawn).astype(jnp.int32)


def draw_adapter_slot(key, part):
    base_key = jax.random.fold_in(key, 11)
    shift_key, turn_key = jax.random.split(base_key, 2)
    owners = MIXTURE_ADAPTERS // ADP_DEV
    indices = jnp.arange(MIXTURE_ADAPTERS, dtype=jnp.int32)
    shift_value = jax.random.randint(shift_key, (), 0, owners)
    turns = jax.random.randint(turn_key, (owners,), 0, ADP_DEV)
    device_of = (indices + shift_value) % owners
    within = (indices // owners + turns[device_of]) % ADP_DEV
    return (device_of * ADP_DEV + within).astype(jnp.int32)


def block_levels(rng, dims, cuts, low, top_value):
    def one(axis_at, shards_of):
        heights = jax.random.uniform(jax.random.fold_in(jax.random.fold_in(rng, 6), axis_at), (shards_of,), jnp.float32, low / len(cuts), top_value / len(cuts))
        return jnp.repeat(jnp.exp(heights), dims[axis_at] // shards_of).reshape((-1,) + (1,) * (len(dims) - axis_at - 1))

    level = one(*cuts[0])
    for cut in cuts[1:]:
        level = level * one(*cut)
    return level


def noise(stream_key, extent, scale, limit, pieces=(), kind=jnp.bfloat16):
    entries = scale * jax.random.normal(stream_key, extent, jnp.float32)
    if pieces:
        entries = entries * block_levels(stream_key, extent, pieces, -0.22, 0.18)
    return jnp.clip(entries, -limit, limit).astype(kind)


def setup_inputs(seed: int = 0) -> dict:
    seeds = jax.random.split(jax.random.key(seed), 8)
    output_gradient = noise(seeds[0], (TOKENS, MODEL_DIM), 16.0, 96.0, ((0, 32), (1, 8)))
    hidden = noise(seeds[1], (TOKENS, HIDDEN_DIM), 0.5, 3.0, ((0, 32), (1, 8)))
    adapter_down = noise(seeds[2], (MIXTURE_ADAPTERS, ADAPTER_RANK, HIDDEN_DIM), HIDDEN_DIM ** -0.5, 0.03125, ((0, 32), (2, 8)))
    adapter_up = noise(seeds[3], (MIXTURE_ADAPTERS, ADAPTER_RANK, MODEL_DIM), MODEL_DIM ** -0.5, 0.0625, ((0, 32), (2, 8)))
    counts = draw_counts(jax.random.fold_in(seeds[7], 71), 0)
    offsets = draw_offsets(jax.random.fold_in(seeds[7], 71), 0)
    adapter_slot = draw_adapter_slot(jax.random.fold_in(seeds[7], 71), 0)
    return dict(output_gradient=output_gradient, hidden=hidden, adapter_down=adapter_down, adapter_up=adapter_up, counts=counts, offsets=offsets, adapter_slot=adapter_slot)


adapter_factor = 2.0


def reference(output_gradient, hidden, adapter_down, adapter_up, counts, offsets, adapter_slot):
    token_count = output_gradient.shape[0]
    adapter_list = adapter_down.shape[0]
    adapter_rank = adapter_down.shape[1]
    hidden_size_count = hidden.shape[1]
    model_feature_width = output_gradient.shape[1]
    rows_per_block = math.gcd(token_count, 1024)
    block_total = token_count // rows_per_block
    down_flattened = adapter_down.reshape(adapter_list * adapter_rank, hidden_size_count)
    up_flattened = adapter_up.reshape(adapter_list * adapter_rank, model_feature_width)
    columns = lax.broadcasted_iota(jnp.int32, (1, adapter_list), 1)
    segment_ends = offsets + counts

    def pick(value_entries, flattened_rows, member_rows_float):
        rank_scores = lax.dot_general(value_entries, flattened_rows, (((1,), (1,)), ((), ())), preferred_element_type=jnp.float32)
        return jnp.sum(rank_scores.reshape(value_entries.shape[0], adapter_list, adapter_rank) * member_rows_float[:, :, None], axis=1)

    def run_block(carry_pair, block_index):
        down_running, up_running = carry_pair
        first_row = block_index * rows_per_block
        grad_block = lax.dynamic_slice_in_dim(output_gradient, first_row, rows_per_block, 0)
        hidden_block = lax.dynamic_slice_in_dim(hidden, first_row, rows_per_block, 0)
        positions = first_row + lax.broadcasted_iota(jnp.int32, (rows_per_block, 1), 0)
        inside = (positions >= offsets[None, :]) & (positions < segment_ends[None, :])
        slot_of_row = jnp.sum(jnp.where(inside, adapter_slot[None, :], 0), axis=1)
        member_rows = (slot_of_row[:, None] == columns).astype(jnp.bfloat16)
        member_rows_float = member_rows.astype(jnp.float32)
        up_incoming = pick(grad_block, up_flattened, member_rows_float).astype(jnp.bfloat16)
        down_incoming = pick(hidden_block, down_flattened, member_rows_float).astype(jnp.bfloat16)
        broadcast_up = (member_rows[:, :, None] * up_incoming[:, None, :]).reshape(rows_per_block, adapter_list * adapter_rank)
        broadcast_down = (member_rows[:, :, None] * down_incoming[:, None, :]).reshape(rows_per_block, adapter_list * adapter_rank)
        hidden_gradient = jnp.dot(broadcast_up, down_flattened, preferred_element_type=jnp.float32)
        hidden_gradient = (adapter_factor * hidden_gradient).astype(jnp.bfloat16)
        down_running = down_running + lax.dot_general(broadcast_up, hidden_block, (((0,), (0,)), ((), ())), preferred_element_type=jnp.float32)
        up_running = up_running + lax.dot_general(broadcast_down, grad_block, (((0,), (0,)), ((), ())), preferred_element_type=jnp.float32)
        return (down_running, up_running), hidden_gradient

    initial_pair = (jnp.zeros((adapter_list * adapter_rank, hidden_size_count), jnp.float32),
                  jnp.zeros((adapter_list * adapter_rank, model_feature_width), jnp.float32))
    (down_running, up_running), grad_blocks = lax.scan(run_block, initial_pair, jnp.arange(block_total, dtype=jnp.int32))
    adapter_hidden_gradient = grad_blocks.reshape(token_count, hidden_size_count)
    slot_grid = adapter_slot[:, None] == columns
    total_slots = jnp.sum(jnp.where(slot_grid, counts[:, None], 0), axis=0)
    scale_entries = adapter_factor / total_slots.astype(jnp.float32)
    adapter_down_gradient = down_running.reshape(adapter_list, adapter_rank, hidden_size_count) * scale_entries[:, None, None]
    adapter_up_gradient = up_running.reshape(adapter_list, adapter_rank, model_feature_width) * scale_entries[:, None, None]
    return adapter_hidden_gradient, adapter_down_gradient, adapter_up_gradient
```

```python
import jax
import jax.numpy as jnp
from jax import lax
from jax.experimental import pallas as pl
from jax.experimental.pallas import tpu as pltpu
from jax.sharding import PartitionSpec as P

adapter_factor = 2.0
BF = jnp.bfloat16
F32 = jnp.float32
I32 = jnp.int32
DP = 32
TP = 8
SLOTS = 64
RANK = 16
TOK = 256
HID = 3584
FEA = 1024
QH = HID // 4
QF = FEA // 4
ROW = QH + QF
LO = 640
HI = ROW - LO
NINE = 256
WIDE = ROW + NINE
LIMIT = 48 * 1024 * 1024


def iota(shape, axis):
    return lax.broadcasted_iota(I32, shape, axis)


def one_hot(condition):
    return jnp.where(condition, 1.0, 0.0).astype(BF)


def dot(a, b, ca=1, cb=0):
    return lax.dot_general(a, b, (((ca,), (cb,)), ((), ())), preferred_element_type=F32)


def tables_kernel(dp_ref, off_ref, cnt_ref, slot_ref, tab_ref, mine_ref, scale_ref):
    dp = dp_ref[0]
    i = iota((8, 640), 1)
    main = i < 512
    d = jnp.where(main, i >> 4, i & 31)
    k = jnp.where(main, (i >> 1) & 7, 8)
    first = d * TOK

    def count_before(a, low):
        return low + jnp.where(off_ref[a] + cnt_ref[a] <= first, 1, 0)

    wanted = lax.fori_loop(0, SLOTS, count_before, jnp.zeros((8, 640), I32), unroll=8) + k

    p = iota((8, TOK), 1)
    start = dp * TOK

    def collect(a, carry):
        tab, mine, c0, c1 = carry
        off = off_ref[a]
        slot = slot_ref[a]
        hit = (wanted == a) & (off < first + TOK)
        tab = jnp.where(hit, slot, tab)
        mine = mine + jnp.where((off > start) & (off <= start + p), 1, 0)
        c0 = jnp.where(slot == 2 * dp, cnt_ref[a], c0)
        c1 = jnp.where(slot == 2 * dp + 1, cnt_ref[a], c1)
        return tab, mine, c0, c1

    init = (jnp.full((8, 640), -1, I32), jnp.zeros((8, TOK), I32), jnp.int32(1), jnp.int32(1))
    tab, mine, c0, c1 = lax.fori_loop(0, SLOTS, collect, init, unroll=8)
    tab_ref[...] = tab
    mine_ref[...] = mine
    rows = iota((32, 128), 0)
    scale_ref[...] = adapter_factor / jnp.where(rows < 16, c0, c1).astype(F32)


def travel_order():
    i = iota((256, 256), 0)
    j = iota((256, 256), 1)
    rp, q, s, r, h = i >> 5, (i >> 3) & 3, (i >> 2) & 1, (i >> 1) & 1, i & 1
    return one_hot(j == q * 64 + h * 32 + s * 16 + rp * 2 + r)


def cut_kernel(down_ref, up_ref, out_ref):
    parts = []
    for q in range(4):
        parts.append(down_ref[:, q * QH : q * QH + LO])
        parts.append(
            jnp.concatenate(
                [
                    down_ref[:, q * QH + LO : (q + 1) * QH],
                    up_ref[:, q * QF : (q + 1) * QF],
                    jnp.zeros((32, LO - HI), BF),
                ],
                axis=1,
            )
        )
    out_ref[...] = dot(travel_order(), jnp.concatenate(parts, axis=0)).astype(BF)


def slot_hits(tab_row, part):
    n = tab_row.shape[1]
    i = iota((256, n), 0)
    c = iota((256, n), 1)
    r = c & 1 if n == 512 else c >> 5
    return one_hot(((i >> 2) == tab_row) & (((i >> 1) & 1) == r) & ((i & 1) == part))


def load_nine(ref, nine):
    nine[:512, :] = ref[:, ROW : ROW + 128].astype(F32)
    nine[512:, :] = ref[:, ROW + 128 :].astype(F32)


def store_nine(nine, ref):
    ref[:, ROW : ROW + 128] = nine[:512, :].astype(BF)
    ref[:, ROW + 128 :] = nine[512:, :].astype(BF)


def pick_kernel(tab_ref, in_ref, out_ref, nine):
    low = in_ref[...]
    high = in_ref[:, :HI]
    main = tab_ref[0:1, 0:512]
    last = tab_ref[0:1, 512:576]
    out_ref[:, :LO] = dot(slot_hits(main, 0), low, 0, 0).astype(BF)
    out_ref[:, LO:ROW] = dot(slot_hits(main, 1), high, 0, 0).astype(BF)
    x = jnp.concatenate(
        [dot(slot_hits(last, 0), low, 0, 0), dot(slot_hits(last, 1), high, 0, 0)], axis=1
    )
    nine[...] = jnp.zeros_like(nine)
    for r in range(2):
        for t in range(9):
            lane, row = divmod(r * 9 + t, 16)
            nine[pl.ds(lane * 512 + row, 32, stride=16), :] = x[
                r * 32 : (r + 1) * 32, t * 128 : (t + 1) * 128
            ]
    store_nine(nine, out_ref)


def unpack_maps(in_ref, nine, maps):
    load_nine(in_ref, nine)
    for q in range(4):
        for rp in range(8):
            at = rp * 64 + q * 16
            maps[q, rp * 16 : rp * 16 + 16, :] = in_ref[at : at + 16, :ROW]
        for t in range(9):
            both = []
            for r in range(2):
                lane, row = divmod(r * 9 + t, 16)
                both.append(nine[pl.ds(lane * 512 + q * 16 + row, 8, stride=64), :])
            maps[q, 128:144, t * 128 : (t + 1) * 128] = jnp.concatenate(both, axis=0).astype(BF)


def row_members(mine):
    i = iota((144, TOK), 0)
    k = jnp.where(i < 128, (i >> 1) & 7, 8)
    return k == mine


def rank_rows():
    o = iota((RANK, 144), 0)
    i = iota((RANK, 144), 1)
    return jnp.where(i < 128, (i & 1) * 8 + (i >> 4), i - 128) == o


def score_kernel(in_ref, hid_ref, grad_ref, mine_ref, out_ref, nine, maps):
    unpack_maps(in_ref, nine, maps)
    up = jnp.zeros((144, TOK), F32)
    down = jnp.zeros((144, TOK), F32)
    for q in range(4):
        down += dot(maps[q, :, :QH], hid_ref[:, q * QH : (q + 1) * QH], 1, 1)
        up += dot(maps[q, :, QH:], grad_ref[:, q * QF : (q + 1) * QF], 1, 1)
    member = row_members(mine_ref[0:1, :])
    fold = jnp.where(rank_rows(), 1.0, 0.0)
    both = [
        lax.dot_general(
            fold,
            jnp.where(member, part, 0.0),
            (((1,), (0,)), ((), ())),
            preferred_element_type=F32,
            precision=lax.Precision.HIGHEST,
        )
        for part in (up, down)
    ]
    block = jnp.concatenate(both, axis=0).astype(BF)
    for z in range(TP):
        out_ref[z * 32 : (z + 1) * 32, :] = block


def gradient_kernel(sig_ref, in_ref, hid_ref, grad_ref, mine_ref, hidden_out, out_ref, nine, maps):
    unpack_maps(in_ref, nine, maps)
    total = sig_ref[0:32, :].astype(F32)
    for z in range(1, TP):
        total += sig_ref[z * 32 : (z + 1) * 32, :].astype(F32)
    signal = total.astype(BF)
    member = row_members(mine_ref[0:1, :])
    fold = one_hot(rank_rows())
    up = jnp.where(member, dot(fold, signal[:RANK], 0, 0), 0.0).astype(BF)
    down = jnp.where(member, dot(fold, signal[RANK:], 0, 0), 0.0).astype(BF)
    nine[...] = jnp.zeros_like(nine)
    for q in range(4):
        hid = hid_ref[:, q * QH : (q + 1) * QH]
        hidden_out[:, q * QH : (q + 1) * QH] = (
            adapter_factor * dot(up, maps[q, :, :QH], 0, 0)
        ).astype(BF)
        sums = jnp.concatenate([dot(up, hid), dot(down, grad_ref[:, q * QF : (q + 1) * QF])], axis=1)
        for rp in range(8):
            at = rp * 64 + q * 16
            out_ref[at : at + 16, :ROW] = sums[rp * 16 : rp * 16 + 16, :].astype(BF)
        for r in range(2):
            for t in range(9):
                lane, row = divmod(r * 9 + t, 16)
                nine[pl.ds(lane * 512 + q * 16 + row, 8, stride=64), :] = sums[
                    128 + r * 8 : 136 + r * 8, t * 128 : (t + 1) * 128
                ]
    store_nine(nine, out_ref)


def reduce_kernel(tab_ref, in_ref, out_ref, nine):
    load_nine(in_ref, nine)
    rows = []
    for r in range(2):
        tiles = []
        for t in range(9):
            lane, row = divmod(r * 9 + t, 16)
            tiles.append(nine[pl.ds(lane * 512 + row, 32, stride=16), :])
        rows.append(jnp.concatenate(tiles, axis=1))
    last = jnp.concatenate(rows, axis=0).astype(BF)
    tab = tab_ref[0:1, 0:512]
    tab9 = tab_ref[0:1, 512:576]
    low = dot(slot_hits(tab, 0), in_ref[:, :LO]) + dot(slot_hits(tab9, 0), last[:, :LO])
    high = dot(slot_hits(tab, 1), in_ref[:, LO:ROW]) + dot(slot_hits(tab9, 1), last[:, LO:])
    out_ref[:, :HI] = (low[:, :HI] + high).astype(BF)
    out_ref[:, HI:] = low[:, HI:].astype(BF)


def join_kernel(scale_ref, in_ref, down_ref, up_ref):
    rows = dot(travel_order(), in_ref[...], 0, 0)
    scale = scale_ref[:, 0:1]
    for q in range(4):
        low = rows[q * 64 : q * 64 + 32, :] * scale
        high = rows[q * 64 + 32 : q * 64 + 64, :] * scale
        down_ref[:, q * QH : q * QH + LO] = low
        down_ref[:, q * QH + LO : (q + 1) * QH] = high[:, : QH - LO]
        up_ref[:, q * QF : (q + 1) * QF] = high[:, QH - LO : HI]


def call(kernel, name, outs, scratch, *args, smem=0):
    vmem = pl.BlockSpec(memory_space=pltpu.VMEM)
    scalar = pl.BlockSpec(memory_space=pltpu.SMEM)
    return pl.pallas_call(
        kernel,
        name=name,
        out_shape=[jax.ShapeDtypeStruct(s, t) for s, t in outs],
        in_specs=[scalar] * smem + [vmem] * (len(args) - smem),
        out_specs=[vmem] * len(outs),
        scratch_shapes=[pltpu.VMEM(s, t) for s, t in scratch],
        compiler_params=pltpu.CompilerParams(vmem_limit_bytes=LIMIT),
    )(*args)


def exchange(x, axis, parts):
    block = x.reshape(parts, x.shape[0] // parts, x.shape[1])
    return lax.all_to_all(block, axis, 0, 0, tiled=True).reshape(x.shape)


def on_device(output_gradient, hidden, adapter_down, adapter_up, counts, offsets, adapter_slot):
    dp = lax.axis_index("dp").astype(I32).reshape(1)
    down = adapter_down.reshape(2 * RANK, HID)
    up = adapter_up.reshape(2 * RANK, FEA)
    (cut,) = call(cut_kernel, "cut", [((256, LO), BF)], [], down, up)
    pieces = exchange(cut, "dp", DP)
    tab, mine, scale = call(
        tables_kernel,
        "tables",
        [((8, 640), I32), ((8, TOK), I32), ((32, 128), F32)],
        [],
        dp,
        offsets,
        counts,
        adapter_slot,
        smem=4,
    )
    nine = ((2 * 512, 128), F32)
    maps = ((4, 144, ROW), BF)
    (picked,) = call(pick_kernel, "pick", [((512, WIDE), BF)], [nine], tab, pieces)
    local = exchange(picked, "dp", DP)
    (partial,) = call(
        score_kernel,
        "score",
        [((TP * 32, TOK), BF)],
        [nine, maps],
        local,
        hidden,
        output_gradient,
        mine,
    )
    signals = exchange(partial, "tensor", TP)
    hidden_gradient, sums = call(
        gradient_kernel,
        "gradient",
        [((TOK, HID), BF), ((512, WIDE), BF)],
        [nine, maps],
        signals,
        local,
        hidden,
        output_gradient,
        mine,
    )
    gathered = exchange(sums, "dp", DP)
    (slot_sums,) = call(reduce_kernel, "reduce", [((256, LO), BF)], [nine], tab, gathered)
    owned = exchange(slot_sums, "dp", DP)
    down_gradient, up_gradient = call(
        join_kernel, "join", [((32, HID), F32), ((32, FEA), F32)], [], scale, owned
    )
    return (
        hidden_gradient,
        down_gradient.reshape(2, RANK, HID),
        up_gradient.reshape(2, RANK, FEA),
    )


def solution(mesh):
    placed = (
        P("dp", "tensor"),
        P("dp", "tensor"),
        P("dp", None, "tensor"),
        P("dp", None, "tensor"),
        P(),
        P(),
        P(),
    )
    return jax.shard_map(
        on_device,
        mesh=mesh,
        in_specs=placed,
        out_specs=(P("dp", "tensor"), P("dp", None, "tensor"), P("dp", None, "tensor")),
        check_vma=False,
    )
```

```python
import jax
import jax.numpy as jnp
from jax import lax
from jax.experimental import pallas as pl
from jax.experimental.pallas import tpu as pltpu
from jax.sharding import PartitionSpec as P

adapter_factor = 2.0
BF = jnp.bfloat16
F32 = jnp.float32
I32 = jnp.int32
DP = 32
TP = 8
SLOTS = 64
RANK = 16
TOK = 256
HID = 3584
FEA = 1024
QH = HID // 4
QF = FEA // 4
ROW = QH + QF
LO = 640
HI = ROW - LO
BLOCK = 168
LIMIT = 48 * 1024 * 1024


def iota(shape, axis):
    return lax.broadcasted_iota(I32, shape, axis)


def one_hot(condition):
    return jnp.where(condition, 1.0, 0.0).astype(BF)


def dot(a, b, ca=1, cb=0):
    return lax.dot_general(a, b, (((ca,), (cb,)), ((), ())), preferred_element_type=F32)


def tables_kernel(dp_ref, off_ref, cnt_ref, slot_ref, tab_ref, mine_ref, scale_ref):
    dp = dp_ref[0]
    i = iota((8, 640), 1)
    main = i < 512
    d = jnp.where(main, i >> 4, i & 31)
    k = jnp.where(main, (i >> 1) & 7, 8)
    first = d * TOK

    def count_before(a, low):
        return low + jnp.where(off_ref[a] + cnt_ref[a] <= first, 1, 0)

    wanted = lax.fori_loop(0, SLOTS, count_before, jnp.zeros((8, 640), I32), unroll=8) + k

    p = iota((8, TOK), 1)
    start = dp * TOK

    def collect(a, carry):
        tab, mine, c0, c1 = carry
        off = off_ref[a]
        slot = slot_ref[a]
        hit = (wanted == a) & (off < first + TOK)
        tab = jnp.where(hit, slot, tab)
        mine = mine + jnp.where((off > start) & (off <= start + p), 1, 0)
        c0 = jnp.where(slot == 2 * dp, cnt_ref[a], c0)
        c1 = jnp.where(slot == 2 * dp + 1, cnt_ref[a], c1)
        return tab, mine, c0, c1

    init = (jnp.full((8, 640), -1, I32), jnp.zeros((8, TOK), I32), jnp.int32(1), jnp.int32(1))
    tab, mine, c0, c1 = lax.fori_loop(0, SLOTS, collect, init, unroll=8)
    tab_ref[...] = tab
    mine_ref[...] = mine
    rows = iota((32, 128), 0)
    scale_ref[...] = adapter_factor / jnp.where(rows < 16, c0, c1).astype(F32)


def travel_order(first, count):
    i = iota((256, count), 0)
    j = iota((256, count), 1) + first
    rp, q, s, r, h = i >> 5, (i >> 3) & 3, (i >> 2) & 1, (i >> 1) & 1, i & 1
    return one_hot(j == q * 64 + h * 32 + s * 16 + rp * 2 + r)


def cut_kernel(down_hbm, up_hbm, out_ref, down_ref, up_ref, sems):
    copies = [
        pltpu.make_async_copy(down_hbm, down_ref, sems.at[0]),
        pltpu.make_async_copy(up_hbm, up_ref, sems.at[1]),
    ]
    for copy in copies:
        copy.start()
    order = travel_order(0, 256)
    for copy in copies:
        copy.wait()
    parts = []
    for q in range(4):
        parts.append(down_ref[:, q * QH : q * QH + LO])
        parts.append(
            jnp.concatenate(
                [
                    down_ref[:, q * QH + LO : (q + 1) * QH],
                    up_ref[:, q * QF : (q + 1) * QF],
                    jnp.zeros((32, LO - HI), BF),
                ],
                axis=1,
            )
        )
    out_ref[...] = dot(order, jnp.concatenate(parts, axis=0)).astype(BF)


def slot_hits(tab_row, part):
    n = tab_row.shape[1]
    i = iota((256, n), 0)
    c = iota((256, n), 1)
    r = c & 1 if n == 512 else c >> 5
    return one_hot(((i >> 2) == tab_row) & (((i >> 1) & 1) == r) & ((i & 1) == part))


def tile_at(block, t):
    return pl.ds(block * BLOCK + t * 16, 16)


def load_nine(ref, nine):
    for b in range(DP):
        nine[b * 24 : b * 24 + 24, :] = ref[b * BLOCK + 144 : (b + 1) * BLOCK, :].astype(F32)


def store_nine(nine, ref):
    for b in range(DP):
        ref[b * BLOCK + 144 : (b + 1) * BLOCK, :] = nine[b * 24 : b * 24 + 24, :].astype(BF)


def pick_kernel(tab_ref, in_ref, out_ref, nine):
    low = in_ref[...]
    high = in_ref[:, :HI]
    main = tab_ref[0:1, 0:512]
    last = tab_ref[0:1, 512:576]
    for part, first, source in ((0, 0, low), (1, LO // 128, high)):
        rows = dot(slot_hits(main, part), source, 0, 0).astype(BF)
        ninth = dot(slot_hits(last, part), source, 0, 0)
        for t in range(source.shape[1] // 128):
            lanes = slice(t * 128, (t + 1) * 128)
            for b in range(DP):
                out_ref[tile_at(b, first + t), :] = rows[b * 16 : b * 16 + 16, lanes]
            for r in range(2):
                nine[pl.ds(r * 9 + first + t, DP, stride=24), :] = ninth[r * 32 : r * 32 + 32, lanes]
    for row in range(18, 24):
        nine[pl.ds(row, DP, stride=24), :] = jnp.zeros((DP, 128), F32)
    store_nine(nine, out_ref)


def unpack_maps(in_ref, nine, maps):
    load_nine(in_ref, nine)
    for q in range(4):
        for t in range(9):
            lanes = slice(t * 128, (t + 1) * 128)
            for rp in range(8):
                maps[q, rp * 16 : rp * 16 + 16, lanes] = in_ref[tile_at(rp * 4 + q, t), :]
            both = [nine[pl.ds(q * 24 + r * 9 + t, 8, stride=96), :] for r in range(2)]
            maps[q, 128:144, lanes] = jnp.concatenate(both, axis=0).astype(BF)


def row_members(mine):
    i = iota((144, TOK), 0)
    k = jnp.where(i < 128, (i >> 1) & 7, 8)
    return k == mine


def rank_rows():
    o = iota((RANK, 144), 0)
    i = iota((RANK, 144), 1)
    return jnp.where(i < 128, (i & 1) * 8 + (i >> 4), i - 128) == o


def score_kernel(in_ref, hid_ref, grad_ref, mine_ref, out_ref, nine, maps):
    unpack_maps(in_ref, nine, maps)
    up = jnp.zeros((144, TOK), F32)
    down = jnp.zeros((144, TOK), F32)
    for q in range(4):
        down += dot(maps[q, :, :QH], hid_ref[:, q * QH : (q + 1) * QH], 1, 1)
        up += dot(maps[q, :, QH:], grad_ref[:, q * QF : (q + 1) * QF], 1, 1)
    member = row_members(mine_ref[0:1, :])
    fold = jnp.where(rank_rows(), 1.0, 0.0)
    both = [
        lax.dot_general(
            fold,
            jnp.where(member, part, 0.0),
            (((1,), (0,)), ((), ())),
            preferred_element_type=F32,
            precision=lax.Precision.HIGHEST,
        )
        for part in (up, down)
    ]
    block = jnp.concatenate(both, axis=0).astype(BF)
    for z in range(TP):
        out_ref[z * 32 : (z + 1) * 32, :] = block


def spread_signal(sig_ref, mine_ref, first):
    total = sig_ref[first : first + RANK, :].astype(F32)
    for z in range(1, TP):
        total += sig_ref[z * 32 + first : z * 32 + first + RANK, :].astype(F32)
    rows = dot(one_hot(rank_rows()), total.astype(BF), 0, 0)
    return jnp.where(row_members(mine_ref[0:1, :]), rows, 0.0).astype(BF)


def sum_kernel(sig_ref, hid_ref, grad_ref, mine_ref, out_ref, nine):
    up = spread_signal(sig_ref, mine_ref, 0)
    down = spread_signal(sig_ref, mine_ref, RANK)
    for q in range(4):
        both = (
            (0, dot(up, hid_ref[:, q * QH : (q + 1) * QH])),
            (7, dot(down, grad_ref[:, q * QF : (q + 1) * QF])),
        )
        for first, sums in both:
            for t in range(sums.shape[1] // 128):
                tile = sums[:, t * 128 : (t + 1) * 128]
                for rp in range(8):
                    out_ref[tile_at(rp * 4 + q, first + t), :] = tile[
                        rp * 16 : rp * 16 + 16, :
                    ].astype(BF)
                for r in range(2):
                    nine[pl.ds(q * 24 + r * 9 + first + t, 8, stride=96), :] = tile[
                        128 + r * 8 : 136 + r * 8, :
                    ]
    for row in range(18, 24):
        nine[pl.ds(row, DP, stride=24), :] = jnp.zeros((DP, 128), F32)
    store_nine(nine, out_ref)


def hidden_kernel(sig_ref, in_ref, mine_ref, out_ref, nine, maps):
    unpack_maps(in_ref, nine, maps)
    up = spread_signal(sig_ref, mine_ref, 0)
    for q in range(4):
        out_ref[:, q * QH : (q + 1) * QH] = (
            adapter_factor * dot(up, maps[q, :, :QH], 0, 0)
        ).astype(BF)


def reduce_kernel(tab_ref, in_ref, out_ref, nine):
    load_nine(in_ref, nine)

    def columns(first, last):
        main, ninth = [], []
        for t in range(first, last):
            main.append(jnp.concatenate([in_ref[tile_at(b, t), :] for b in range(DP)], axis=0))
            rows = [nine[pl.ds(r * 9 + t, DP, stride=24), :] for r in range(2)]
            ninth.append(jnp.concatenate(rows, axis=0).astype(BF))
        return jnp.concatenate(main, axis=1), jnp.concatenate(ninth, axis=1)

    def summed(part, first, last):
        main, ninth = columns(first, last)
        return dot(slot_hits(tab_ref[0:1, 0:512], part), main) + dot(
            slot_hits(tab_ref[0:1, 512:576], part), ninth
        )

    low = summed(0, 0, LO // 128)
    high = summed(1, LO // 128, 9)
    out_ref[:, :HI] = (low[:, :HI] + high).astype(BF)
    out_ref[:, HI:] = low[:, HI:].astype(BF)


def join_kernel(scale_ref, in_ref, down_hbm, up_hbm, down_ref, up_ref, sems):
    scale = scale_ref[:, 0:1]
    pieces = in_ref[...]
    copies = []
    for q in range(4):
        rows = dot(travel_order(q * 64, 64), pieces, 0, 0)
        low = rows[:32, :] * scale
        high = rows[32:, :] * scale
        down_ref[:, q * QH : q * QH + LO] = low
        down_ref[:, q * QH + LO : (q + 1) * QH] = high[:, : QH - LO]
        up_ref[:, q * QF : (q + 1) * QF] = high[:, QH - LO : HI]
        lanes = pl.ds(q * QH, QH)
        copies.append(
            pltpu.make_async_copy(down_ref.at[:, lanes], down_hbm.at[:, lanes], sems.at[q])
        )
        lanes = pl.ds(q * QF, QF)
        copies.append(pltpu.make_async_copy(up_ref.at[:, lanes], up_hbm.at[:, lanes], sems.at[4 + q]))
        for copy in copies[-2:]:
            copy.start()
    for copy in copies:
        copy.wait()


def call(kernel, name, outs, scratch, *args, smem=0, hbm_in=0, hbm_out=False, limit=LIMIT):
    vmem = pl.BlockSpec(memory_space=pltpu.VMEM)
    scalar = pl.BlockSpec(memory_space=pltpu.SMEM)
    hbm = pl.BlockSpec(memory_space=pltpu.HBM)
    return pl.pallas_call(
        kernel,
        name=name,
        out_shape=[jax.ShapeDtypeStruct(s, t) for s, t in outs],
        in_specs=[scalar] * smem + [hbm] * hbm_in + [vmem] * (len(args) - smem - hbm_in),
        out_specs=[hbm if hbm_out else vmem] * len(outs),
        scratch_shapes=scratch,
        compiler_params=pltpu.CompilerParams(vmem_limit_bytes=limit),
    )(*args)


def exchange(x, axis, parts):
    block = x.reshape(parts, x.shape[0] // parts, x.shape[1])
    return lax.all_to_all(block, axis, 0, 0, tiled=True).reshape(x.shape)


def on_device(output_gradient, hidden, adapter_down, adapter_up, counts, offsets, adapter_slot):
    dp = lax.axis_index("dp").astype(I32).reshape(1)
    down = adapter_down.reshape(2 * RANK, HID)
    up = adapter_up.reshape(2 * RANK, FEA)
    (cut,) = call(
        cut_kernel,
        "cut",
        [((256, LO), BF)],
        [
            pltpu.VMEM((32, HID), BF),
            pltpu.VMEM((32, FEA), BF),
            pltpu.SemaphoreType.DMA((2,)),
        ],
        down,
        up,
        hbm_in=2,
        limit=63_400_000,
    )
    pieces = exchange(cut, "dp", DP)
    tab, mine, scale = call(
        tables_kernel,
        "tables",
        [((8, 640), I32), ((8, TOK), I32), ((32, 128), F32)],
        [],
        dp,
        offsets,
        counts,
        adapter_slot,
        smem=4,
    )
    nine = pltpu.VMEM((DP * 24, 128), F32)
    maps = pltpu.VMEM((4, 144, ROW), BF)
    block = ((DP * BLOCK, 128), BF)
    (picked,) = call(pick_kernel, "pick", [block], [nine], tab, pieces)
    local = exchange(picked, "dp", DP)
    (partial,) = call(
        score_kernel,
        "score",
        [((TP * 32, TOK), BF)],
        [nine, maps],
        local,
        hidden,
        output_gradient,
        mine,
    )
    signals = exchange(partial, "tensor", TP)
    (sums,) = call(sum_kernel, "sums", [block], [nine], signals, hidden, output_gradient, mine)
    gathered = exchange(sums, "dp", DP)
    (hidden_gradient,) = call(
        hidden_kernel, "hidden", [((TOK, HID), BF)], [nine, maps], signals, local, mine
    )
    (slot_sums,) = call(reduce_kernel, "reduce", [((256, LO), BF)], [nine], tab, gathered)
    owned = exchange(slot_sums, "dp", DP)
    down_gradient, up_gradient = call(
        join_kernel,
        "join",
        [((32, HID), F32), ((32, FEA), F32)],
        [
            pltpu.VMEM((32, HID), F32),
            pltpu.VMEM((32, FEA), F32),
            pltpu.SemaphoreType.DMA((8,)),
        ],
        scale,
        owned,
        hbm_out=True,
    )
    return (
        hidden_gradient,
        down_gradient.reshape(2, RANK, HID),
        up_gradient.reshape(2, RANK, FEA),
    )


def solution(mesh):
    placed = (
        P("dp", "tensor"),
        P("dp", "tensor"),
        P("dp", None, "tensor"),
        P("dp", None, "tensor"),
        P(),
        P(),
        P(),
    )
    return jax.shard_map(
        on_device,
        mesh=mesh,
        in_specs=placed,
        out_specs=(P("dp", "tensor"), P("dp", None, "tensor"), P("dp", None, "tensor")),
        check_vma=False,
    )
```

```python
import jax
import jax.numpy as jnp
from jax import lax
from jax.experimental import pallas as pl
from jax.experimental.pallas import tpu as pltpu
from jax.sharding import PartitionSpec as P

adapter_factor = 2.0
BF = jnp.bfloat16
F32 = jnp.float32
I32 = jnp.int32
DP = 32
TP = 8
SLOTS = 64
RANK = 16
TOK = 256
HID = 3584
FEA = 1024
QH = HID // 4
QF = FEA // 4
ROW = QH + QF
LO = 640
HI = ROW - LO
EXTRA = 32
SIG = 96
LIMIT = 16 * 1024 * 1024


def iota(shape, axis):
    return lax.broadcasted_iota(I32, shape, axis)


def one_hot(condition):
    return jnp.where(condition, 1.0, 0.0).astype(BF)


def dot(a, b, ca=1, cb=0):
    return lax.dot_general(a, b, (((ca,), (cb,)), ((), ())), preferred_element_type=F32)


def tables_kernel(dp_ref, off_ref, cnt_ref, slot_ref, tab_ref, mine_ref, scale_ref):
    dp = dp_ref[0]
    i = iota((8, 512), 1)
    first = (i >> 4) * TOK

    def count_before(a, low):
        return low + jnp.where(off_ref[a] + cnt_ref[a] <= first, 1, 0)

    wanted = lax.fori_loop(0, SLOTS, count_before, jnp.zeros((8, 512), I32), unroll=8)
    wanted += (i >> 1) & 7

    p = iota((8, 384), 1)
    own = p < TOK
    start = (dp - jnp.where(own, 0, 1)) * TOK
    at = start + jnp.where(own, p, p - EXTRA)

    def collect(a, carry):
        tab, mine, c0, c1 = carry
        off = off_ref[a]
        slot = slot_ref[a]
        hit = (wanted == a) & (off < first + TOK)
        tab = jnp.where(hit, slot, tab)
        mine = mine + jnp.where((off > start) & (off <= at), 1, 0)
        c0 = jnp.where(slot == 2 * dp, cnt_ref[a], c0)
        c1 = jnp.where(slot == 2 * dp + 1, cnt_ref[a], c1)
        return tab, mine, c0, c1

    init = (jnp.full((8, 512), -1, I32), jnp.zeros((8, 384), I32), jnp.int32(1), jnp.int32(1))
    tab, mine, c0, c1 = lax.fori_loop(0, SLOTS, collect, init, unroll=8)
    tab_ref[...] = tab
    extra = (p < TOK + EXTRA) & (mine == 8)
    mine_ref[...] = jnp.where(own, mine, jnp.where(extra, 0, -1))
    rows = iota((32, 128), 0)
    scale_ref[...] = adapter_factor / jnp.where(rows < 16, c0, c1).astype(F32)


def travel_order(first, count):
    i = iota((256, count), 0)
    j = iota((256, count), 1) + first
    rp, q, s, r, h = i >> 5, (i >> 3) & 3, (i >> 2) & 1, (i >> 1) & 1, i & 1
    return one_hot(j == q * 64 + h * 32 + s * 16 + rp * 2 + r)


def cut_kernel(down_hbm, up_hbm, out_ref, down_ref, up_ref, sems):
    copies = [
        pltpu.make_async_copy(down_hbm, down_ref, sems.at[0]),
        pltpu.make_async_copy(up_hbm, up_ref, sems.at[1]),
    ]
    for copy in copies:
        copy.start()
    order = travel_order(0, 256)
    for copy in copies:
        copy.wait()
    parts = []
    for q in range(4):
        parts.append(down_ref[:, q * QH : q * QH + LO])
        parts.append(
            jnp.concatenate(
                [
                    down_ref[:, q * QH + LO : (q + 1) * QH],
                    up_ref[:, q * QF : (q + 1) * QF],
                    jnp.zeros((32, LO - HI), BF),
                ],
                axis=1,
            )
        )
    out_ref[...] = dot(order, jnp.concatenate(parts, axis=0)).astype(BF)


def slot_hits(tab_ref, part):
    i = iota((256, 512), 0)
    r = iota((256, 512), 1) & 1
    return one_hot(((i >> 2) == tab_ref[0:1, :]) & (((i >> 1) & 1) == r) & ((i & 1) == part))


def pick_kernel(tab_ref, in_ref, after_ref, out_ref):
    out_ref[:, :LO] = dot(slot_hits(tab_ref, 0), in_ref[...], 0, 0).astype(BF)
    out_ref[:, LO:] = dot(slot_hits(tab_ref, 1), in_ref[:, :HI], 0, 0).astype(BF)


def quarter(ref, q, lanes):
    tiles = [ref[(rp * 4 + q) * 16 : (rp * 4 + q) * 16 + 16, lanes] for rp in range(8)]
    return jnp.concatenate(tiles, axis=0)


def members(mine_ref):
    k = (iota((128, TOK), 0) >> 1) & 7
    own = k == mine_ref[0:1, :TOK]
    k = (iota((128, EXTRA), 0) >> 1) & 7
    return own, k == mine_ref[0:1, TOK : TOK + EXTRA]


def rank_rows():
    o = iota((RANK, 128), 0)
    i = iota((RANK, 128), 1)
    return (i & 1) * 8 + (i >> 4) == o


def score_kernel(in_ref, hid_ref, grad_ref, extra_ref, mine_ref, out_ref):
    own_up = jnp.zeros((128, TOK), F32)
    own_down = jnp.zeros((128, TOK), F32)
    extra_up = jnp.zeros((128, EXTRA), F32)
    extra_down = jnp.zeros((128, EXTRA), F32)
    for q in range(4):
        lanes = slice(q * QH, (q + 1) * QH)
        part = quarter(in_ref, q, slice(0, QH))
        own_down += dot(part, hid_ref[:, lanes], 1, 1)
        extra_down += dot(part, extra_ref[:, lanes], 1, 1)
        lanes = slice(q * QF, (q + 1) * QF)
        part = quarter(in_ref, q, slice(QH, ROW))
        own_up += dot(part, grad_ref[:, lanes], 1, 1)
        extra_up += dot(part, extra_ref[:, HID + q * QF : HID + (q + 1) * QF], 1, 1)
    own, extra = members(mine_ref)
    fold = jnp.where(rank_rows(), 1.0, 0.0)

    def folded(member, up, down):
        return [
            lax.dot_general(
                fold,
                jnp.where(member, part, 0.0),
                (((1,), (0,)), ((), ())),
                preferred_element_type=F32,
                precision=lax.Precision.HIGHEST,
            )
            for part in (up, down)
        ]

    block = jnp.concatenate(folded(own, own_up, own_down), axis=0).astype(BF)
    tail = jnp.concatenate(folded(extra, extra_up, extra_down), axis=0).astype(BF)
    tail = jnp.concatenate([tail, jnp.zeros((32, 128 - EXTRA), BF)], axis=1)
    block = jnp.concatenate([block[:, :128], block[:, 128:], tail], axis=0)
    for z in range(TP):
        out_ref[z * SIG : (z + 1) * SIG, :] = block


def spread_signal(sig_ref, mine_ref, first):
    parts = []
    for base in (0, 32, 64):
        at = base + first
        total = sig_ref[at : at + RANK, :].astype(F32)
        for z in range(1, TP):
            total += sig_ref[z * SIG + at : z * SIG + at + RANK, :].astype(F32)
        parts.append(total.astype(BF))
    own, extra = members(mine_ref)
    fold = one_hot(rank_rows())
    rows = dot(fold, jnp.concatenate(parts[:2], axis=1), 0, 0)
    tail = dot(fold, parts[2], 0, 0)[:, :EXTRA]
    return jnp.where(own, rows, 0.0).astype(BF), jnp.where(extra, tail, 0.0).astype(BF)


def sum_kernel(sig_ref, hid_ref, grad_ref, extra_ref, mine_ref, out_ref):
    up, up_extra = spread_signal(sig_ref, mine_ref, 0)
    down, down_extra = spread_signal(sig_ref, mine_ref, RANK)
    for q in range(4):
        lanes = slice(q * QH, (q + 1) * QH)
        sums = dot(up, hid_ref[:, lanes]) + dot(up_extra, extra_ref[:, lanes])
        for rp in range(8):
            at = (rp * 4 + q) * 16
            out_ref[at : at + 16, :QH] = sums[rp * 16 : rp * 16 + 16, :].astype(BF)
        sums = dot(down, grad_ref[:, q * QF : (q + 1) * QF]) + dot(
            down_extra, extra_ref[:, HID + q * QF : HID + (q + 1) * QF]
        )
        for rp in range(8):
            at = (rp * 4 + q) * 16
            out_ref[at : at + 16, QH:] = sums[rp * 16 : rp * 16 + 16, :].astype(BF)


def extra_kernel(sig_ref, in_ref, mine_ref, out_ref):
    _, up = spread_signal(sig_ref, mine_ref, 0)
    for q in range(4):
        out_ref[:, q * QH : (q + 1) * QH] = (
            adapter_factor * dot(up, quarter(in_ref, q, slice(0, QH)), 0, 0)
        ).astype(BF)


def hidden_kernel(sig_ref, in_ref, mine_ref, back_ref, out_ref):
    up, _ = spread_signal(sig_ref, mine_ref, 0)
    cut = TOK - EXTRA
    for q in range(4):
        lanes = slice(q * QH, (q + 1) * QH)
        rows = adapter_factor * dot(up, quarter(in_ref, q, slice(0, QH)), 0, 0)
        out_ref[:cut, lanes] = rows[:cut, :].astype(BF)
        out_ref[cut:, lanes] = (rows[cut:, :] + back_ref[:, lanes].astype(F32)).astype(BF)


def reduce_kernel(tab_ref, in_ref, out_ref):
    low = dot(slot_hits(tab_ref, 0), in_ref[:, :LO])
    high = dot(slot_hits(tab_ref, 1), in_ref[:, LO:])
    out_ref[:, :HI] = (low[:, :HI] + high).astype(BF)
    out_ref[:, HI:] = low[:, HI:].astype(BF)


def join_kernel(scale_ref, in_ref, down_hbm, up_hbm, down_ref, up_ref, sems):
    scale = scale_ref[:, 0:1]
    pieces = in_ref[...]
    copies = []
    for q in range(4):
        rows = dot(travel_order(q * 64, 64), pieces, 0, 0)
        low = rows[:32, :] * scale
        high = rows[32:, :] * scale
        down_ref[:, q * QH : q * QH + LO] = low
        down_ref[:, q * QH + LO : (q + 1) * QH] = high[:, : QH - LO]
        up_ref[:, q * QF : (q + 1) * QF] = high[:, QH - LO : HI]
        lanes = pl.ds(q * QH, QH)
        copies.append(
            pltpu.make_async_copy(down_ref.at[:, lanes], down_hbm.at[:, lanes], sems.at[q])
        )
        lanes = pl.ds(q * QF, QF)
        copies.append(pltpu.make_async_copy(up_ref.at[:, lanes], up_hbm.at[:, lanes], sems.at[4 + q]))
        for copy in copies[-2:]:
            copy.start()
    for copy in copies:
        copy.wait()


def call(kernel, name, outs, scratch, *args, smem=0, hbm_in=0, any_in=0, hbm_out=False, limit=LIMIT):
    vmem = pl.BlockSpec(memory_space=pltpu.VMEM)
    scalar = pl.BlockSpec(memory_space=pltpu.SMEM)
    hbm = pl.BlockSpec(memory_space=pltpu.HBM)
    return pl.pallas_call(
        kernel,
        name=name,
        out_shape=[jax.ShapeDtypeStruct(s, t) for s, t in outs],
        in_specs=[scalar] * smem + [hbm] * hbm_in
        + [vmem] * (len(args) - smem - hbm_in - any_in)
        + [pl.BlockSpec(memory_space=pl.ANY)] * any_in,
        out_specs=[hbm if hbm_out else vmem] * len(outs),
        scratch_shapes=scratch,
        compiler_params=pltpu.CompilerParams(vmem_limit_bytes=limit),
    )(*args)


def exchange(x, axis, parts):
    block = x.reshape(parts, x.shape[0] // parts, x.shape[1])
    return lax.all_to_all(block, axis, 0, 0, tiled=True).reshape(x.shape)


def on_device(output_gradient, hidden, adapter_down, adapter_up, counts, offsets, adapter_slot):
    dp = lax.axis_index("dp").astype(I32).reshape(1)
    onward = [(i, i + 1) for i in range(DP - 1)]
    backward = [(i + 1, i) for i in range(DP - 1)]
    last = jnp.concatenate([hidden[TOK - EXTRA :], output_gradient[TOK - EXTRA :]], axis=1)
    extra = lax.ppermute(last, "dp", onward)
    down = adapter_down.reshape(2 * RANK, HID)
    up = adapter_up.reshape(2 * RANK, FEA)
    (cut,) = call(
        cut_kernel,
        "cut",
        [((256, LO), BF)],
        [
            pltpu.VMEM((32, HID), BF),
            pltpu.VMEM((32, FEA), BF),
            pltpu.SemaphoreType.DMA((2,)),
        ],
        down,
        up,
        hbm_in=2,
        limit=63_400_000,
    )
    pieces = exchange(cut, "dp", DP)
    tab, mine, scale = call(
        tables_kernel,
        "tables",
        [((8, 512), I32), ((8, 384), I32), ((32, 128), F32)],
        [],
        dp,
        offsets,
        counts,
        adapter_slot,
        smem=4,
    )
    block = ((512, ROW), BF)
    (picked,) = call(pick_kernel, "pick", [block], [], tab, pieces, extra, any_in=1)
    local = exchange(picked, "dp", DP)
    tokens = (hidden, output_gradient, extra, mine)
    (partial,) = call(score_kernel, "score", [((TP * SIG, 128), BF)], [], local, *tokens)
    signals = exchange(partial, "tensor", TP)
    (sums,) = call(sum_kernel, "sums", [block], [], signals, *tokens)
    gathered = exchange(sums, "dp", DP)
    (extra_gradient,) = call(
        extra_kernel, "extra", [((EXTRA, HID), BF)], [], signals, local, mine
    )
    back = lax.ppermute(extra_gradient, "dp", backward)
    (hidden_gradient,) = call(
        hidden_kernel, "hidden", [((TOK, HID), BF)], [], signals, local, mine, back
    )
    (slot_sums,) = call(reduce_kernel, "reduce", [((256, LO), BF)], [], tab, gathered)
    owned = exchange(slot_sums, "dp", DP)
    down_gradient, up_gradient = call(
        join_kernel,
        "join",
        [((32, HID), F32), ((32, FEA), F32)],
        [
            pltpu.VMEM((32, HID), F32),
            pltpu.VMEM((32, FEA), F32),
            pltpu.SemaphoreType.DMA((8,)),
        ],
        scale,
        owned,
        hbm_out=True,
    )
    return (
        hidden_gradient,
        down_gradient.reshape(2, RANK, HID),
        up_gradient.reshape(2, RANK, FEA),
    )


def solution(mesh):
    placed = (
        P("dp", "tensor"),
        P("dp", "tensor"),
        P("dp", None, "tensor"),
        P("dp", None, "tensor"),
        P(),
        P(),
        P(),
    )
    return jax.shard_map(
        on_device,
        mesh=mesh,
        in_specs=placed,
        out_specs=(P("dp", "tensor"), P("dp", None, "tensor"), P("dp", None, "tensor")),
        check_vma=False,
    )
```

```python
import jax
import jax.numpy as jnp
from jax import lax
from jax.experimental import pallas as pl
from jax.experimental.pallas import tpu as pltpu
from jax.sharding import PartitionSpec as P


adapter_factor = 2.0
BF = jnp.bfloat16
F32 = jnp.float32
I32 = jnp.int32
DP = 32
TP = 8
SLOTS = 64
RANK = 16
TOK = 256
HID = 3584
FEA = 1024
QH = HID // 4
QF = FEA // 4
ROW = QH + QF
LO = 640
HI = ROW - LO
EXTRA = 32
SIG = 96
LIMIT = 16 * 1024 * 1024


def iota(shape, axis):
    return lax.broadcasted_iota(I32, shape, axis)


def one_hot(condition):
    return jnp.where(condition, 1.0, 0.0).astype(BF)


def dot(a, b, ca=1, cb=0):
    return lax.dot_general(a, b, (((ca,), (cb,)), ((), ())), preferred_element_type=F32)


def tables_kernel(dp_ref, off_ref, cnt_ref, slot_ref, tab_ref, mine_ref, scale_ref):
    dp = dp_ref[0]
    i = iota((8, 512), 1)
    first = (i >> 4) * TOK

    def count_before(a, low):
        return low + jnp.where(off_ref[a] + cnt_ref[a] <= first, 1, 0)

    wanted = lax.fori_loop(0, SLOTS, count_before, jnp.zeros((8, 512), I32), unroll=8)
    wanted += (i >> 1) & 7

    p = iota((8, 384), 1)
    own = p < TOK
    start = (dp - jnp.where(own, 0, 1)) * TOK
    at = start + jnp.where(own, p, p - EXTRA)

    def collect(a, carry):
        tab, mine, c0, c1 = carry
        off = off_ref[a]
        slot = slot_ref[a]
        hit = (wanted == a) & (off < first + TOK)
        tab = jnp.where(hit, slot, tab)
        mine = mine + jnp.where((off > start) & (off <= at), 1, 0)
        c0 = jnp.where(slot == 2 * dp, cnt_ref[a], c0)
        c1 = jnp.where(slot == 2 * dp + 1, cnt_ref[a], c1)
        return tab, mine, c0, c1

    init = (jnp.full((8, 512), -1, I32), jnp.zeros((8, 384), I32), jnp.int32(1), jnp.int32(1))
    tab, mine, c0, c1 = lax.fori_loop(0, SLOTS, collect, init, unroll=8)
    tab_ref[...] = tab
    extra = (p < TOK + EXTRA) & (mine == 8)
    mine_ref[...] = jnp.where(own, mine, jnp.where(extra, 0, -1))
    rows = iota((32, 128), 0)
    scale_ref[...] = adapter_factor / jnp.where(rows < 16, c0, c1).astype(F32)


def travel_order(first, count):
    i = iota((256, count), 0)
    j = iota((256, count), 1) + first
    rp, q, s, r, h = i >> 5, (i >> 3) & 3, (i >> 2) & 1, (i >> 1) & 1, i & 1
    return one_hot(j == q * 64 + h * 32 + s * 16 + rp * 2 + r)


def cut_kernel(down_hbm, up_hbm, out_ref, down_ref, up_ref, sems):
    copies = [
        pltpu.make_async_copy(down_hbm, down_ref, sems.at[0]),
        pltpu.make_async_copy(up_hbm, up_ref, sems.at[1]),
    ]
    for copy in copies:
        copy.start()
    order = travel_order(0, 256)
    for copy in copies:
        copy.wait()
    parts = []
    for q in range(4):
        parts.append(down_ref[:, q * QH : q * QH + LO])
        parts.append(
            jnp.concatenate(
                [
                    down_ref[:, q * QH + LO : (q + 1) * QH],
                    up_ref[:, q * QF : (q + 1) * QF],
                    jnp.zeros((32, LO - HI), BF),
                ],
                axis=1,
            )
        )
    out_ref[...] = dot(order, jnp.concatenate(parts, axis=0)).astype(BF)


def slot_hits(tab_ref, part):
    i = iota((256, 512), 0)
    r = iota((256, 512), 1) & 1
    return one_hot(((i >> 2) == tab_ref[0:1, :]) & (((i >> 1) & 1) == r) & ((i & 1) == part))


def pick_kernel(tab_ref, in_ref, out_ref):
    out_ref[:, :LO] = dot(slot_hits(tab_ref, 0), in_ref[...], 0, 0).astype(BF)
    out_ref[:, LO:] = dot(slot_hits(tab_ref, 1), in_ref[:, :HI], 0, 0).astype(BF)


def quarter(ref, q, lanes):
    tiles = [ref[(rp * 4 + q) * 16 : (rp * 4 + q) * 16 + 16, lanes] for rp in range(8)]
    return jnp.concatenate(tiles, axis=0)


def members(mine_ref):
    k = (iota((128, TOK), 0) >> 1) & 7
    own = k == mine_ref[0:1, :TOK]
    k = (iota((128, EXTRA), 0) >> 1) & 7
    return own, k == mine_ref[0:1, TOK : TOK + EXTRA]


def rank_rows():
    o = iota((RANK, 128), 0)
    i = iota((RANK, 128), 1)
    return (i & 1) * 8 + (i >> 4) == o


def mark_kernel(in_hbm, mine_ref, out_ref):
    out_ref[...] = mine_ref[...]


def score_kernel(in_ref, hid_ref, grad_ref, extra_ref, mine_ref, out_ref):
    own_up = jnp.zeros((128, TOK), F32)
    own_down = jnp.zeros((128, TOK), F32)
    extra_up = jnp.zeros((128, EXTRA), F32)
    extra_down = jnp.zeros((128, EXTRA), F32)
    for q in range(4):
        lanes = slice(q * QH, (q + 1) * QH)
        part = quarter(in_ref, q, slice(0, QH))
        own_down += dot(part, hid_ref[:, lanes], 1, 1)
        extra_down += dot(part, extra_ref[:, lanes], 1, 1)
        lanes = slice(q * QF, (q + 1) * QF)
        part = quarter(in_ref, q, slice(QH, ROW))
        own_up += dot(part, grad_ref[:, lanes], 1, 1)
        extra_up += dot(part, extra_ref[:, HID + q * QF : HID + (q + 1) * QF], 1, 1)
    own, extra = members(mine_ref)
    fold = jnp.where(rank_rows(), 1.0, 0.0)

    def folded(member, up, down):
        return [
            lax.dot_general(
                fold,
                jnp.where(member, part, 0.0),
                (((1,), (0,)), ((), ())),
                preferred_element_type=F32,
                precision=lax.Precision.HIGHEST,
            )
            for part in (up, down)
        ]

    block = jnp.concatenate(folded(own, own_up, own_down), axis=0).astype(BF)
    tail = jnp.concatenate(folded(extra, extra_up, extra_down), axis=0).astype(BF)
    tail = jnp.concatenate([tail, jnp.zeros((32, 128 - EXTRA), BF)], axis=1)
    block = jnp.concatenate([block[:, :128], block[:, 128:], tail], axis=0)
    for z in range(TP):
        out_ref[z * SIG : (z + 1) * SIG, :] = block


def spread_signal(sig_ref, mine_ref, first):
    parts = []
    for base in (0, 32, 64):
        at = base + first
        total = sig_ref[at : at + RANK, :].astype(F32)
        for z in range(1, TP):
            total += sig_ref[z * SIG + at : z * SIG + at + RANK, :].astype(F32)
        parts.append(total.astype(BF))
    own, extra = members(mine_ref)
    fold = one_hot(rank_rows())
    rows = dot(fold, jnp.concatenate(parts[:2], axis=1), 0, 0)
    tail = dot(fold, parts[2], 0, 0)[:, :EXTRA]
    return jnp.where(own, rows, 0.0).astype(BF), jnp.where(extra, tail, 0.0).astype(BF)


def sum_kernel(sig_ref, hid_ref, grad_ref, extra_ref, mine_ref, out_ref):
    up, up_extra = spread_signal(sig_ref, mine_ref, 0)
    down, down_extra = spread_signal(sig_ref, mine_ref, RANK)
    for q in range(4):
        lanes = slice(q * QH, (q + 1) * QH)
        sums = dot(up, hid_ref[:, lanes]) + dot(up_extra, extra_ref[:, lanes])
        for rp in range(8):
            at = (rp * 4 + q) * 16
            out_ref[at : at + 16, :QH] = sums[rp * 16 : rp * 16 + 16, :].astype(BF)
        sums = dot(down, grad_ref[:, q * QF : (q + 1) * QF]) + dot(
            down_extra, extra_ref[:, HID + q * QF : HID + (q + 1) * QF]
        )
        for rp in range(8):
            at = (rp * 4 + q) * 16
            out_ref[at : at + 16, QH:] = sums[rp * 16 : rp * 16 + 16, :].astype(BF)


def extra_kernel(sig_ref, in_ref, mine_ref, out_ref):
    _, up = spread_signal(sig_ref, mine_ref, 0)
    for q in range(4):
        out_ref[:, q * QH : (q + 1) * QH] = (
            adapter_factor * dot(up, quarter(in_ref, q, slice(0, QH)), 0, 0)
        ).astype(BF)


def hidden_kernel(sig_ref, in_ref, mine_ref, out_hbm, tail_ref, head_ref, sems):
    up, _ = spread_signal(sig_ref, mine_ref, 0)
    cut = TOK - EXTRA
    copies = []
    for q in range(4):
        lanes = slice(q * QH, (q + 1) * QH)
        rows = adapter_factor * dot(up, quarter(in_ref, q, slice(0, QH)), 0, 0)
        head_ref[:, lanes] = rows[:cut, :].astype(BF)
        tail_ref[:, lanes] = rows[cut:, :].astype(BF)
        copies.append(
            pltpu.make_async_copy(
                head_ref.at[:, pl.ds(q * QH, QH)],
                out_hbm.at[pl.ds(0, cut), pl.ds(q * QH, QH)],
                sems.at[q],
            )
        )
        copies[-1].start()
    for copy in copies:
        copy.wait()


def reduce_kernel(tab_ref, in_ref, out_ref):
    low = dot(slot_hits(tab_ref, 0), in_ref[:, :LO])
    high = dot(slot_hits(tab_ref, 1), in_ref[:, LO:])
    out_ref[:, :HI] = (low[:, :HI] + high).astype(BF)
    out_ref[:, HI:] = low[:, HI:].astype(BF)


def join_kernel(
    head_hbm,
    scale_ref,
    in_ref,
    tail_ref,
    back_ref,
    hidden_hbm,
    down_hbm,
    up_hbm,
    down_ref,
    up_ref,
    rows_ref,
    sems,
):
    rows_ref[...] = (tail_ref[...].astype(F32) + back_ref[...].astype(F32)).astype(BF)
    copies = [
        pltpu.make_async_copy(
            rows_ref, hidden_hbm.at[pl.ds(TOK - EXTRA, EXTRA), :], sems.at[8]
        )
    ]
    copies[0].start()
    scale = scale_ref[:, 0:1]
    pieces = in_ref[...]
    for q in range(4):
        rows = dot(travel_order(q * 64, 64), pieces, 0, 0)
        low = rows[:32, :] * scale
        high = rows[32:, :] * scale
        down_ref[:, q * QH : q * QH + LO] = low
        down_ref[:, q * QH + LO : (q + 1) * QH] = high[:, : QH - LO]
        up_ref[:, q * QF : (q + 1) * QF] = high[:, QH - LO : HI]
        lanes = pl.ds(q * QH, QH)
        copies.append(
            pltpu.make_async_copy(down_ref.at[:, lanes], down_hbm.at[:, lanes], sems.at[q])
        )
        lanes = pl.ds(q * QF, QF)
        copies.append(pltpu.make_async_copy(up_ref.at[:, lanes], up_hbm.at[:, lanes], sems.at[4 + q]))
        for copy in copies[-2:]:
            copy.start()
    for copy in copies:
        copy.wait()


def call(kernel, outs, scratch, *args, smem=0, any_in=0, hbm_in=0, hbm_out=0, alias=None, limit=LIMIT):
    vmem = pl.BlockSpec(memory_space=pltpu.VMEM)
    scalar = pl.BlockSpec(memory_space=pltpu.SMEM)
    hbm = pl.BlockSpec(memory_space=pltpu.HBM)
    return pl.pallas_call(
        kernel,
        out_shape=[jax.ShapeDtypeStruct(s, t) for s, t in outs],
        in_specs=[scalar] * smem + [pl.BlockSpec(memory_space=pl.ANY)] * any_in
        + [hbm] * hbm_in
        + [vmem] * (len(args) - smem - any_in - hbm_in),
        out_specs=[hbm] * hbm_out + [vmem] * (len(outs) - hbm_out),
        scratch_shapes=scratch,
        input_output_aliases=alias or {},
        compiler_params=pltpu.CompilerParams(vmem_limit_bytes=limit),
    )(*args)


def exchange(x, axis, parts):
    block = x.reshape(parts, x.shape[0] // parts, x.shape[1])
    return lax.all_to_all(block, axis, 0, 0, tiled=True).reshape(x.shape)


def on_device(output_gradient, hidden, adapter_down, adapter_up, counts, offsets, adapter_slot):
    dp = lax.axis_index("dp").astype(I32).reshape(1)
    onward = [(i, i + 1) for i in range(DP - 1)]
    backward = [(i + 1, i) for i in range(DP - 1)]
    last = jnp.concatenate([hidden[TOK - EXTRA :], output_gradient[TOK - EXTRA :]], axis=1)
    extra = lax.ppermute(last, "dp", onward)
    down = adapter_down.reshape(2 * RANK, HID)
    up = adapter_up.reshape(2 * RANK, FEA)
    (cut,) = call(
        cut_kernel,
        [((256, LO), BF)],
        [
            pltpu.VMEM((32, HID), BF),
            pltpu.VMEM((32, FEA), BF),
            pltpu.SemaphoreType.DMA((2,)),
        ],
        down,
        up,
        hbm_in=2,
        limit=63_400_000,
    )
    pieces = exchange(cut, "dp", DP)
    tab, mine, scale = call(
        tables_kernel,
        [((8, 512), I32), ((8, 384), I32), ((32, 128), F32)],
        [],
        dp,
        offsets,
        counts,
        adapter_slot,
        smem=4,
    )
    block = ((512, ROW), BF)
    (picked,) = call(pick_kernel, [block], [], tab, pieces)
    local = exchange(picked, "dp", DP)
    (mine,) = call(mark_kernel, [((8, 384), I32)], [], local, mine, any_in=1)
    tokens = (hidden, output_gradient, extra, mine)
    (partial,) = call(score_kernel, [((TP * SIG, 128), BF)], [], local, *tokens)
    signals = exchange(partial, "tensor", TP)
    (sums,) = call(sum_kernel, [block], [], signals, *tokens)
    gathered = exchange(sums, "dp", DP)
    (extra_gradient,) = call(extra_kernel, [((EXTRA, HID), BF)], [], signals, local, mine)
    back = lax.ppermute(extra_gradient, "dp", backward)
    head, tail = call(
        hidden_kernel,
        [((TOK, HID), BF), ((EXTRA, HID), BF)],
        [pltpu.VMEM((TOK - EXTRA, HID), BF), pltpu.SemaphoreType.DMA((4,))],
        signals,
        local,
        mine,
        hbm_out=1,
    )
    (slot_sums,) = call(reduce_kernel, [((256, LO), BF)], [], tab, gathered)
    owned = exchange(slot_sums, "dp", DP)
    hidden_gradient, down_gradient, up_gradient = call(
        join_kernel,
        [((TOK, HID), BF), ((32, HID), F32), ((32, FEA), F32)],
        [
            pltpu.VMEM((32, HID), F32),
            pltpu.VMEM((32, FEA), F32),
            pltpu.VMEM((EXTRA, HID), BF),
            pltpu.SemaphoreType.DMA((9,)),
        ],
        head,
        scale,
        owned,
        tail,
        back,
        hbm_in=1,
        hbm_out=3,
        alias={0: 0},
    )
    return (
        hidden_gradient,
        down_gradient.reshape(2, RANK, HID),
        up_gradient.reshape(2, RANK, FEA),
    )


def solution(mesh):
    placed = (
        P("dp", "tensor"),
        P("dp", "tensor"),
        P("dp", None, "tensor"),
        P("dp", None, "tensor"),
        P(),
        P(),
        P(),
    )
    return jax.shard_map(
        on_device,
        mesh=mesh,
        in_specs=placed,
        out_specs=(P("dp", "tensor"), P("dp", None, "tensor"), P("dp", None, "tensor")),
        check_vma=False,
    )
```

```python
import jax
import jax.numpy as jnp
from jax import lax
from jax.experimental import pallas as pl
from jax.experimental.pallas import tpu as pltpu
from jax.sharding import PartitionSpec as P


adapter_factor = 2.0
BF = jnp.bfloat16
F32 = jnp.float32
I32 = jnp.int32
DP = 32
TP = 8
SLOTS = 64
RANK = 16
TOK = 256
HID = 3584
FEA = 1024
QH = HID // 4
QF = FEA // 4
ROW = QH + QF
LO = 640
HI = ROW - LO
EXTRA = 32
SIG = 72
LIMIT = 16 * 1024 * 1024


def iota(shape, axis):
    return lax.broadcasted_iota(I32, shape, axis)


def one_hot(condition):
    return jnp.where(condition, 1.0, 0.0).astype(BF)


def dot(a, b, ca=1, cb=0):
    return lax.dot_general(a, b, (((ca,), (cb,)), ((), ())), preferred_element_type=F32)


def tables_kernel(dp_ref, off_ref, cnt_ref, slot_ref, tab_ref, mine_ref, scale_ref):
    dp = dp_ref[0]
    i = iota((8, 512), 1)
    first = (i >> 4) * TOK

    def count_before(a, low):
        return low + jnp.where(off_ref[a] + cnt_ref[a] <= first, 1, 0)

    wanted = lax.fori_loop(0, SLOTS, count_before, jnp.zeros((8, 512), I32), unroll=8)
    wanted += (i >> 1) & 7

    p = iota((8, 384), 1)
    own = p < TOK
    start = (dp - jnp.where(own, 0, 1)) * TOK
    at = start + jnp.where(own, p, p - EXTRA)

    def collect(a, carry):
        tab, mine, c0, c1 = carry
        off = off_ref[a]
        slot = slot_ref[a]
        hit = (wanted == a) & (off < first + TOK)
        tab = jnp.where(hit, slot, tab)
        mine = mine + jnp.where((off > start) & (off <= at), 1, 0)
        c0 = jnp.where(slot == 2 * dp, cnt_ref[a], c0)
        c1 = jnp.where(slot == 2 * dp + 1, cnt_ref[a], c1)
        return tab, mine, c0, c1

    init = (jnp.full((8, 512), -1, I32), jnp.zeros((8, 384), I32), jnp.int32(1), jnp.int32(1))
    tab, mine, c0, c1 = lax.fori_loop(0, SLOTS, collect, init, unroll=8)
    tab_ref[...] = tab
    extra = (p < TOK + EXTRA) & (mine == 8)
    mine_ref[...] = jnp.where(own, mine, jnp.where(extra, 0, -1))
    rows = iota((32, 128), 0)
    scale_ref[...] = adapter_factor / jnp.where(rows < 16, c0, c1).astype(F32)


def travel_order(first, count):
    i = iota((256, count), 0)
    j = iota((256, count), 1) + first
    rp, q, s, r, h = i >> 5, (i >> 3) & 3, (i >> 2) & 1, (i >> 1) & 1, i & 1
    return one_hot(j == q * 64 + h * 32 + s * 16 + rp * 2 + r)


def cut_kernel(down_hbm, up_hbm, out_ref, down_ref, up_ref, sems):
    copies = [
        pltpu.make_async_copy(down_hbm, down_ref, sems.at[0]),
        pltpu.make_async_copy(up_hbm, up_ref, sems.at[1]),
    ]
    for copy in copies:
        copy.start()
    order = travel_order(0, 256)
    for copy in copies:
        copy.wait()
    parts = []
    for q in range(4):
        parts.append(down_ref[:, q * QH : q * QH + LO])
        parts.append(
            jnp.concatenate(
                [
                    down_ref[:, q * QH + LO : (q + 1) * QH],
                    up_ref[:, q * QF : (q + 1) * QF],
                    jnp.zeros((32, LO - HI), BF),
                ],
                axis=1,
            )
        )
    out_ref[...] = dot(order, jnp.concatenate(parts, axis=0)).astype(BF)


def slot_hits(tab_ref, part):
    i = iota((256, 512), 0)
    r = iota((256, 512), 1) & 1
    return one_hot(((i >> 2) == tab_ref[0:1, :]) & (((i >> 1) & 1) == r) & ((i & 1) == part))


def pick_kernel(tab_ref, in_ref, out_ref):
    out_ref[:, :LO] = dot(slot_hits(tab_ref, 0), in_ref[...], 0, 0).astype(BF)
    out_ref[:, LO:] = dot(slot_hits(tab_ref, 1), in_ref[:, :HI], 0, 0).astype(BF)


def quarter(ref, q, lanes):
    tiles = [ref[(rp * 4 + q) * 16 : (rp * 4 + q) * 16 + 16, lanes] for rp in range(8)]
    return jnp.concatenate(tiles, axis=0)


def members(mine_ref):
    k = (iota((128, TOK), 0) >> 1) & 7
    own = k == mine_ref[0:1, :TOK]
    k = (iota((128, EXTRA), 0) >> 1) & 7
    return own, k == mine_ref[0:1, TOK : TOK + EXTRA]


def rank_rows():
    o = iota((RANK, 128), 0)
    i = iota((RANK, 128), 1)
    return (i & 1) * 8 + (i >> 4) == o


def mark_kernel(in_hbm, mine_ref, grad_ref, out_ref):
    out_ref[...] = mine_ref[...]


def score_kernel(grad_ref, in_ref, hid_ref, extra_ref, mine_ref, out_ref):
    own_up = jnp.zeros((128, TOK), F32)
    own_down = jnp.zeros((128, TOK), F32)
    extra_up = jnp.zeros((128, EXTRA), F32)
    extra_down = jnp.zeros((128, EXTRA), F32)
    for q in range(4):
        lanes = slice(q * QH, (q + 1) * QH)
        part = quarter(in_ref, q, slice(0, QH))
        own_down += dot(part, hid_ref[:, lanes], 1, 1)
        extra_down += dot(part, extra_ref[:, lanes], 1, 1)
    for q in range(4):
        lanes = slice(q * QF, (q + 1) * QF)
        part = quarter(in_ref, q, slice(QH, ROW))
        own_up += dot(part, grad_ref[:, lanes], 1, 1)
        extra_up += dot(part, extra_ref[:, HID + q * QF : HID + (q + 1) * QF], 1, 1)
    own, extra = members(mine_ref)
    fold = jnp.where(rank_rows(), 1.0, 0.0)

    def folded(member, up, down):
        return [
            lax.dot_general(
                fold,
                jnp.where(member, part, 0.0),
                (((1,), (0,)), ((), ())),
                preferred_element_type=F32,
                precision=lax.Precision.HIGHEST,
            )
            for part in (up, down)
        ]

    block = jnp.concatenate(folded(own, own_up, own_down), axis=0).astype(BF)
    tail = jnp.concatenate(folded(extra, extra_up, extra_down), axis=0)
    tail = jnp.concatenate([tail[i * 8 : i * 8 + 8, :] for i in range(4)], axis=1).astype(BF)
    for z in range(TP):
        out_ref[z * SIG : z * SIG + 32, :] = block[:, :128]
        out_ref[z * SIG + 32 : z * SIG + 64, :] = block[:, 128:]
        out_ref[z * SIG + 64 : (z + 1) * SIG, :] = tail


def spread_signal(sig_ref, mine_ref, first):
    def total(at, rows):
        part = sig_ref[at : at + rows, :].astype(F32)
        for z in range(1, TP):
            part += sig_ref[z * SIG + at : z * SIG + at + rows, :].astype(F32)
        return part

    tail = total(64, 8)
    at = first * 4
    tail = jnp.concatenate(
        [tail[:, at : at + EXTRA], tail[:, at + EXTRA : at + 2 * EXTRA]], axis=0
    )
    parts = [total(first, RANK), total(32 + first, RANK)]
    own, extra = members(mine_ref)
    fold = one_hot(rank_rows())
    rows = dot(fold, jnp.concatenate(parts, axis=1).astype(BF), 0, 0)
    tail = dot(fold, tail.astype(BF), 0, 0)
    return jnp.where(own, rows, 0.0).astype(BF), jnp.where(extra, tail, 0.0).astype(BF)


def sum_kernel(grad_ref, sig_ref, hid_ref, extra_ref, mine_ref, out_ref):
    up, up_extra = spread_signal(sig_ref, mine_ref, 0)
    for q in range(4):
        lanes = slice(q * QH, (q + 1) * QH)
        sums = dot(up, hid_ref[:, lanes]) + dot(up_extra, extra_ref[:, lanes])
        for rp in range(8):
            at = (rp * 4 + q) * 16
            out_ref[at : at + 16, :QH] = sums[rp * 16 : rp * 16 + 16, :].astype(BF)
    down, down_extra = spread_signal(sig_ref, mine_ref, RANK)
    for q in range(4):
        sums = dot(down, grad_ref[:, q * QF : (q + 1) * QF]) + dot(
            down_extra, extra_ref[:, HID + q * QF : HID + (q + 1) * QF]
        )
        for rp in range(8):
            at = (rp * 4 + q) * 16
            out_ref[at : at + 16, QH:] = sums[rp * 16 : rp * 16 + 16, :].astype(BF)


def extra_kernel(sig_ref, in_ref, mine_ref, out_ref):
    _, up = spread_signal(sig_ref, mine_ref, 0)
    for q in range(4):
        out_ref[:, q * QH : (q + 1) * QH] = (
            adapter_factor * dot(up, quarter(in_ref, q, slice(0, QH)), 0, 0)
        ).astype(BF)


def hidden_kernel(sig_ref, in_ref, mine_ref, out_hbm, tail_ref, head_ref, sems):
    up, _ = spread_signal(sig_ref, mine_ref, 0)
    cut = TOK - EXTRA
    copies = []
    for q in range(4):
        lanes = slice(q * QH, (q + 1) * QH)
        rows = adapter_factor * dot(up, quarter(in_ref, q, slice(0, QH)), 0, 0)
        head_ref[:, lanes] = rows[:cut, :].astype(BF)
        tail_ref[:, lanes] = rows[cut:, :].astype(BF)
        copies.append(
            pltpu.make_async_copy(
                head_ref.at[:, pl.ds(q * QH, QH)],
                out_hbm.at[pl.ds(0, cut), pl.ds(q * QH, QH)],
                sems.at[q],
            )
        )
        copies[-1].start()
    for copy in copies:
        copy.wait()


def reduce_kernel(tab_ref, in_ref, out_ref):
    low = dot(slot_hits(tab_ref, 0), in_ref[:, :LO])
    high = dot(slot_hits(tab_ref, 1), in_ref[:, LO:])
    out_ref[:, :HI] = (low[:, :HI] + high).astype(BF)
    out_ref[:, HI:] = low[:, HI:].astype(BF)


def join_kernel(
    head_hbm,
    scale_ref,
    in_ref,
    tail_ref,
    back_ref,
    hidden_hbm,
    down_hbm,
    up_hbm,
    down_ref,
    up_ref,
    rows_ref,
    sems,
):
    rows_ref[...] = (tail_ref[...].astype(F32) + back_ref[...].astype(F32)).astype(BF)
    copies = [
        pltpu.make_async_copy(
            rows_ref, hidden_hbm.at[pl.ds(TOK - EXTRA, EXTRA), :], sems.at[8]
        )
    ]
    copies[0].start()
    scale = scale_ref[:, 0:1]
    pieces = in_ref[...]
    for q in range(4):
        rows = dot(travel_order(q * 64, 64), pieces, 0, 0)
        low = rows[:32, :] * scale
        high = rows[32:, :] * scale
        down_ref[:, q * QH : q * QH + LO] = low
        down_ref[:, q * QH + LO : (q + 1) * QH] = high[:, : QH - LO]
        up_ref[:, q * QF : (q + 1) * QF] = high[:, QH - LO : HI]
        lanes = pl.ds(q * QH, QH)
        copies.append(
            pltpu.make_async_copy(down_ref.at[:, lanes], down_hbm.at[:, lanes], sems.at[q])
        )
        lanes = pl.ds(q * QF, QF)
        copies.append(pltpu.make_async_copy(up_ref.at[:, lanes], up_hbm.at[:, lanes], sems.at[4 + q]))
        for copy in copies[-2:]:
            copy.start()
    for copy in copies:
        copy.wait()


def call(kernel, outs, scratch, *args, smem=0, any_in=0, hbm_in=0, hbm_out=0, alias=None, limit=LIMIT):
    vmem = pl.BlockSpec(memory_space=pltpu.VMEM)
    scalar = pl.BlockSpec(memory_space=pltpu.SMEM)
    hbm = pl.BlockSpec(memory_space=pltpu.HBM)
    return pl.pallas_call(
        kernel,
        out_shape=[jax.ShapeDtypeStruct(s, t) for s, t in outs],
        in_specs=[scalar] * smem + [pl.BlockSpec(memory_space=pl.ANY)] * any_in
        + [hbm] * hbm_in
        + [vmem] * (len(args) - smem - any_in - hbm_in),
        out_specs=[hbm] * hbm_out + [vmem] * (len(outs) - hbm_out),
        scratch_shapes=scratch,
        input_output_aliases=alias or {},
        compiler_params=pltpu.CompilerParams(vmem_limit_bytes=limit),
    )(*args)


def exchange(x, axis, parts):
    block = x.reshape(parts, x.shape[0] // parts, x.shape[1])
    return lax.all_to_all(block, axis, 0, 0, tiled=True).reshape(x.shape)


def on_device(output_gradient, hidden, adapter_down, adapter_up, counts, offsets, adapter_slot):
    dp = lax.axis_index("dp").astype(I32).reshape(1)
    onward = [(i, i + 1) for i in range(DP - 1)]
    backward = [(i + 1, i) for i in range(DP - 1)]
    last = jnp.concatenate([hidden[TOK - EXTRA :], output_gradient[TOK - EXTRA :]], axis=1)
    extra = lax.ppermute(last, "dp", onward)
    down = adapter_down.reshape(2 * RANK, HID)
    up = adapter_up.reshape(2 * RANK, FEA)
    (cut,) = call(
        cut_kernel,
        [((256, LO), BF)],
        [
            pltpu.VMEM((32, HID), BF),
            pltpu.VMEM((32, FEA), BF),
            pltpu.SemaphoreType.DMA((2,)),
        ],
        down,
        up,
        hbm_in=2,
        limit=63_400_000,
    )
    pieces = exchange(cut, "dp", DP)
    tab, mine, scale = call(
        tables_kernel,
        [((8, 512), I32), ((8, 384), I32), ((32, 128), F32)],
        [],
        dp,
        offsets,
        counts,
        adapter_slot,
        smem=4,
    )
    block = ((512, ROW), BF)
    (picked,) = call(pick_kernel, [block], [], tab, pieces)
    local = exchange(picked, "dp", DP)
    (mine,) = call(mark_kernel, [((8, 384), I32)], [], local, mine, output_gradient, any_in=1)
    tokens = (hidden, extra, mine)
    (partial,) = call(score_kernel, [((TP * SIG, 128), BF)], [], output_gradient, local, *tokens)
    signals = exchange(partial, "tensor", TP)
    (sums,) = call(sum_kernel, [block], [], output_gradient, signals, *tokens)
    gathered = exchange(sums, "dp", DP)
    (extra_gradient,) = call(extra_kernel, [((EXTRA, HID), BF)], [], signals, local, mine)
    back = lax.ppermute(extra_gradient, "dp", backward)
    head, tail = call(
        hidden_kernel,
        [((TOK, HID), BF), ((EXTRA, HID), BF)],
        [pltpu.VMEM((TOK - EXTRA, HID), BF), pltpu.SemaphoreType.DMA((4,))],
        signals,
        local,
        mine,
        hbm_out=1,
    )
    (slot_sums,) = call(reduce_kernel, [((256, LO), BF)], [], tab, gathered)
    owned = exchange(slot_sums, "dp", DP)
    hidden_gradient, down_gradient, up_gradient = call(
        join_kernel,
        [((TOK, HID), BF), ((32, HID), F32), ((32, FEA), F32)],
        [
            pltpu.VMEM((32, HID), F32),
            pltpu.VMEM((32, FEA), F32),
            pltpu.VMEM((EXTRA, HID), BF),
            pltpu.SemaphoreType.DMA((9,)),
        ],
        head,
        scale,
        owned,
        tail,
        back,
        hbm_in=1,
        hbm_out=3,
        alias={0: 0},
    )
    return (
        hidden_gradient,
        down_gradient.reshape(2, RANK, HID),
        up_gradient.reshape(2, RANK, FEA),
    )


def solution(mesh):
    placed = (
        P("dp", "tensor"),
        P("dp", "tensor"),
        P("dp", None, "tensor"),
        P("dp", None, "tensor"),
        P(),
        P(),
        P(),
    )
    return jax.shard_map(
        on_device,
        mesh=mesh,
        in_specs=placed,
        out_specs=(P("dp", "tensor"), P("dp", None, "tensor"), P("dp", None, "tensor")),
        check_vma=False,
    )
```

```python
import jax
import jax.numpy as jnp
from jax import lax
from jax.experimental import pallas as pl
from jax.experimental.pallas import tpu as pltpu
from jax.sharding import PartitionSpec as P


adapter_factor = 2.0
BF = jnp.bfloat16
F32 = jnp.float32
I32 = jnp.int32
DP = 32
TP = 8
SLOTS = 64
RANK = 16
TOK = 256
HID = 3584
FEA = 1024
QH = HID // 4
QF = FEA // 4
ROW = QH + QF
LO = 640
HI = ROW - LO
EXTRA = 32
SIG = 72
LIMIT = 16 * 1024 * 1024


def iota(shape, axis):
    return lax.broadcasted_iota(I32, shape, axis)


def one_hot(condition):
    return jnp.where(condition, 1.0, 0.0).astype(BF)


def dot(a, b, ca=1, cb=0):
    return lax.dot_general(a, b, (((ca,), (cb,)), ((), ())), preferred_element_type=F32)


def tables_kernel(dp_ref, off_ref, cnt_ref, slot_ref, tab_ref, mine_ref, scale_ref):
    dp = dp_ref[0]
    i = iota((8, 512), 1)
    first = (i >> 4) * TOK

    def count_before(a, low):
        return low + jnp.where(off_ref[a] + cnt_ref[a] <= first, 1, 0)

    wanted = lax.fori_loop(0, SLOTS, count_before, jnp.zeros((8, 512), I32), unroll=8)
    wanted += (i >> 1) & 7

    p = iota((8, 384), 1)
    own = p < TOK
    start = (dp - jnp.where(own, 0, 1)) * TOK
    at = start + jnp.where(own, p, p - EXTRA)

    def collect(a, carry):
        tab, mine, c0, c1 = carry
        off = off_ref[a]
        slot = slot_ref[a]
        hit = (wanted == a) & (off < first + TOK)
        tab = jnp.where(hit, slot, tab)
        mine = mine + jnp.where((off > start) & (off <= at), 1, 0)
        c0 = jnp.where(slot == 2 * dp, cnt_ref[a], c0)
        c1 = jnp.where(slot == 2 * dp + 1, cnt_ref[a], c1)
        return tab, mine, c0, c1

    init = (jnp.full((8, 512), -1, I32), jnp.zeros((8, 384), I32), jnp.int32(1), jnp.int32(1))
    tab, mine, c0, c1 = lax.fori_loop(0, SLOTS, collect, init, unroll=8)
    tab_ref[...] = tab
    extra = (p < TOK + EXTRA) & (mine == 8)
    mine_ref[...] = jnp.where(own, mine, jnp.where(extra, 0, -1))
    rows = iota((32, 128), 0)
    scale_ref[...] = adapter_factor / jnp.where(rows < 16, c0, c1).astype(F32)


def travel_order(first, count):
    i = iota((256, count), 0)
    j = iota((256, count), 1) + first
    rp, q, s, r, h = i >> 5, (i >> 3) & 3, (i >> 2) & 1, (i >> 1) & 1, i & 1
    return one_hot(j == q * 64 + h * 32 + s * 16 + rp * 2 + r)


def store_parts(value, out_ref, out_hbm, sems, first):
    copies = []
    for n, at in enumerate((0, 256, 512)):
        width = min(256, LO - at)
        out_ref[:, at : at + width] = value(slice(at, at + width)).astype(BF)
        lanes = pl.ds(at, width)
        copies.append(
            pltpu.make_async_copy(out_ref.at[:, lanes], out_hbm.at[:, lanes], sems.at[first + n])
        )
        copies[-1].start()
    for copy in copies:
        copy.wait()


def cut_kernel(down_hbm, up_hbm, out_hbm, down_ref, up_ref, out_ref, sems):
    copies = [
        pltpu.make_async_copy(down_hbm, down_ref, sems.at[0]),
        pltpu.make_async_copy(up_hbm, up_ref, sems.at[1]),
    ]
    for copy in copies:
        copy.start()
    order = travel_order(0, 256)
    for copy in copies:
        copy.wait()
    parts = []
    for q in range(4):
        parts.append(down_ref[:, q * QH : q * QH + LO])
        parts.append(
            jnp.concatenate(
                [
                    down_ref[:, q * QH + LO : (q + 1) * QH],
                    up_ref[:, q * QF : (q + 1) * QF],
                    jnp.zeros((32, LO - HI), BF),
                ],
                axis=1,
            )
        )
    parts = jnp.concatenate(parts, axis=0)
    store_parts(lambda lanes: dot(order, parts[:, lanes]), out_ref, out_hbm, sems, 2)


def slot_hits(tab_ref, part):
    i = iota((256, 512), 0)
    r = iota((256, 512), 1) & 1
    return one_hot(((i >> 2) == tab_ref[0:1, :]) & (((i >> 1) & 1) == r) & ((i & 1) == part))


def pick_kernel(tab_ref, in_ref, out_ref):
    out_ref[:, :LO] = dot(slot_hits(tab_ref, 0), in_ref[...], 0, 0).astype(BF)
    out_ref[:, LO:] = dot(slot_hits(tab_ref, 1), in_ref[:, :HI], 0, 0).astype(BF)


def quarter(ref, q, lanes):
    tiles = [ref[(rp * 4 + q) * 16 : (rp * 4 + q) * 16 + 16, lanes] for rp in range(8)]
    return jnp.concatenate(tiles, axis=0)


def members(mine_ref):
    k = (iota((128, TOK), 0) >> 1) & 7
    own = k == mine_ref[0:1, :TOK]
    k = (iota((128, EXTRA), 0) >> 1) & 7
    return own, k == mine_ref[0:1, TOK : TOK + EXTRA]


def rank_rows():
    o = iota((RANK, 128), 0)
    i = iota((RANK, 128), 1)
    return (i & 1) * 8 + (i >> 4) == o


def mark_kernel(in_hbm, mine_ref, grad_ref, out_ref):
    out_ref[...] = mine_ref[...]


def score_kernel(grad_ref, in_ref, hid_ref, extra_ref, mine_ref, out_ref):
    up = jnp.zeros((TOK + EXTRA, 128), F32)
    down = jnp.zeros((TOK + EXTRA, 128), F32)
    for q in range(4):
        lanes = slice(q * QH, (q + 1) * QH)
        tokens = jnp.concatenate([hid_ref[:, lanes], extra_ref[:, lanes]], axis=0)
        down += dot(tokens, quarter(in_ref, q, slice(0, QH)), 1, 1)
        lanes = slice(q * QF, (q + 1) * QF)
        behind = slice(HID + q * QF, HID + (q + 1) * QF)
        tokens = jnp.concatenate([grad_ref[:, lanes], extra_ref[:, behind]], axis=0)
        up += dot(tokens, quarter(in_ref, q, slice(QH, ROW)), 1, 1)
    mine = mine_ref[:, : TOK + EXTRA].astype(F32).astype(BF)
    mine = dot(mine, jnp.full((8, 128), 0.125, BF), 0, 0)
    member = ((iota((TOK + EXTRA, 128), 1) >> 1) & 7).astype(F32) == mine
    fold = jnp.where(rank_rows(), 1.0, 0.0)
    rows = jnp.concatenate(
        [
            lax.dot_general(
                fold,
                jnp.where(member, part, 0.0),
                (((1,), (1,)), ((), ())),
                preferred_element_type=F32,
                precision=lax.Precision.HIGHEST,
            )
            for part in (up, down)
        ],
        axis=0,
    )
    block = rows.astype(BF)
    tail = rows[:, TOK:]
    tail = jnp.concatenate([tail[i * 8 : i * 8 + 8, :] for i in range(4)], axis=1).astype(BF)
    for z in range(TP):
        out_ref[z * SIG : z * SIG + 32, :] = block[:, :128]
        out_ref[z * SIG + 32 : z * SIG + 64, :] = block[:, 128:TOK]
        out_ref[z * SIG + 64 : (z + 1) * SIG, :] = tail


def spread_signal(sig_ref, mine_ref, first):
    def total(at, rows):
        part = sig_ref[at : at + rows, :].astype(F32)
        for z in range(1, TP):
            part += sig_ref[z * SIG + at : z * SIG + at + rows, :].astype(F32)
        return part

    tail = total(64, 8)
    at = first * 4
    tail = jnp.concatenate(
        [tail[:, at : at + EXTRA], tail[:, at + EXTRA : at + 2 * EXTRA]], axis=0
    )
    parts = [total(first, RANK), total(32 + first, RANK)]
    own, extra = members(mine_ref)
    fold = one_hot(rank_rows())
    rows = dot(fold, jnp.concatenate(parts, axis=1).astype(BF), 0, 0)
    tail = dot(fold, tail.astype(BF), 0, 0)
    return jnp.where(own, rows, 0.0).astype(BF), jnp.where(extra, tail, 0.0).astype(BF)


def sum_kernel(grad_ref, sig_ref, hid_ref, extra_ref, mine_ref, out_ref):
    up = jnp.concatenate(spread_signal(sig_ref, mine_ref, 0), axis=1)
    down = jnp.concatenate(spread_signal(sig_ref, mine_ref, RANK), axis=1)
    for q in range(4):
        lanes = slice(q * QH, (q + 1) * QH)
        tokens = jnp.concatenate([hid_ref[:, lanes], extra_ref[:, lanes]], axis=0)
        sums = dot(up, tokens)
        for rp in range(8):
            at = (rp * 4 + q) * 16
            out_ref[at : at + 16, :QH] = sums[rp * 16 : rp * 16 + 16, :].astype(BF)
        lanes = slice(q * QF, (q + 1) * QF)
        behind = slice(HID + q * QF, HID + (q + 1) * QF)
        tokens = jnp.concatenate([grad_ref[:, lanes], extra_ref[:, behind]], axis=0)
        sums = dot(down, tokens)
        for rp in range(8):
            at = (rp * 4 + q) * 16
            out_ref[at : at + 16, QH:] = sums[rp * 16 : rp * 16 + 16, :].astype(BF)


def extra_kernel(sig_ref, in_ref, mine_ref, out_ref):
    _, up = spread_signal(sig_ref, mine_ref, 0)
    for q in range(4):
        out_ref[:, q * QH : (q + 1) * QH] = (
            adapter_factor * dot(up, quarter(in_ref, q, slice(0, QH)), 0, 0)
        ).astype(BF)


def hidden_kernel(sig_ref, in_ref, mine_ref, out_hbm, tail_ref, head_ref, sems):
    up, _ = spread_signal(sig_ref, mine_ref, 0)
    cut = TOK - EXTRA
    copies = []
    for q in range(4):
        lanes = slice(q * QH, (q + 1) * QH)
        rows = adapter_factor * dot(up, quarter(in_ref, q, slice(0, QH)), 0, 0)
        head_ref[:, lanes] = rows[:cut, :].astype(BF)
        tail_ref[:, lanes] = rows[cut:, :].astype(BF)
        copies.append(
            pltpu.make_async_copy(
                head_ref.at[:, pl.ds(q * QH, QH)],
                out_hbm.at[pl.ds(0, cut), pl.ds(q * QH, QH)],
                sems.at[q],
            )
        )
        copies[-1].start()
    for copy in copies:
        copy.wait()


def reduce_kernel(tab_ref, in_ref, out_hbm, out_ref, sems):
    hits = [slot_hits(tab_ref, 0), slot_hits(tab_ref, 1)]

    def value(lanes):
        sums = dot(hits[0], in_ref[:, lanes])
        if lanes.start < HI:
            sums += dot(hits[1], in_ref[:, LO + lanes.start : LO + lanes.stop])
        return sums

    store_parts(value, out_ref, out_hbm, sems, 0)


def join_kernel(
    head_hbm,
    scale_ref,
    in_ref,
    tail_ref,
    back_ref,
    hidden_hbm,
    down_hbm,
    up_hbm,
    down_ref,
    up_ref,
    rows_ref,
    sems,
):
    rows_ref[...] = (tail_ref[...].astype(F32) + back_ref[...].astype(F32)).astype(BF)
    copies = [
        pltpu.make_async_copy(
            rows_ref, hidden_hbm.at[pl.ds(TOK - EXTRA, EXTRA), :], sems.at[8]
        )
    ]
    copies[0].start()
    scale = scale_ref[:, 0:1]
    pieces = in_ref[...]
    for q in range(4):
        rows = dot(travel_order(q * 64, 64), pieces, 0, 0)
        low = rows[:32, :] * scale
        high = rows[32:, :] * scale
        down_ref[:, q * QH : q * QH + LO] = low
        down_ref[:, q * QH + LO : (q + 1) * QH] = high[:, : QH - LO]
        up_ref[:, q * QF : (q + 1) * QF] = high[:, QH - LO : HI]
        lanes = pl.ds(q * QH, QH)
        copies.append(
            pltpu.make_async_copy(down_ref.at[:, lanes], down_hbm.at[:, lanes], sems.at[q])
        )
        lanes = pl.ds(q * QF, QF)
        copies.append(pltpu.make_async_copy(up_ref.at[:, lanes], up_hbm.at[:, lanes], sems.at[4 + q]))
        for copy in copies[-2:]:
            copy.start()
    for copy in copies:
        copy.wait()


def call(kernel, outs, scratch, *args, smem=0, any_in=0, hbm_in=0, hbm_out=0, alias=None, limit=LIMIT):
    vmem = pl.BlockSpec(memory_space=pltpu.VMEM)
    scalar = pl.BlockSpec(memory_space=pltpu.SMEM)
    hbm = pl.BlockSpec(memory_space=pltpu.HBM)
    return pl.pallas_call(
        kernel,
        out_shape=[jax.ShapeDtypeStruct(s, t) for s, t in outs],
        in_specs=[scalar] * smem + [pl.BlockSpec(memory_space=pl.ANY)] * any_in
        + [hbm] * hbm_in
        + [vmem] * (len(args) - smem - any_in - hbm_in),
        out_specs=[hbm] * hbm_out + [vmem] * (len(outs) - hbm_out),
        scratch_shapes=scratch,
        input_output_aliases=alias or {},
        compiler_params=pltpu.CompilerParams(vmem_limit_bytes=limit),
    )(*args)


def exchange(x, axis, parts):
    block = x.reshape(parts, x.shape[0] // parts, x.shape[1])
    return lax.all_to_all(block, axis, 0, 0, tiled=True).reshape(x.shape)


def on_device(output_gradient, hidden, adapter_down, adapter_up, counts, offsets, adapter_slot):
    dp = lax.axis_index("dp").astype(I32).reshape(1)
    onward = [(i, i + 1) for i in range(DP - 1)]
    backward = [(i + 1, i) for i in range(DP - 1)]
    last = jnp.concatenate([hidden[TOK - EXTRA :], output_gradient[TOK - EXTRA :]], axis=1)
    extra = lax.ppermute(last, "dp", onward)
    down = adapter_down.reshape(2 * RANK, HID)
    up = adapter_up.reshape(2 * RANK, FEA)
    (cut,) = call(
        cut_kernel,
        [((256, LO), BF)],
        [
            pltpu.VMEM((32, HID), BF),
            pltpu.VMEM((32, FEA), BF),
            pltpu.VMEM((256, LO), BF),
            pltpu.SemaphoreType.DMA((5,)),
        ],
        down,
        up,
        hbm_in=2,
        hbm_out=1,
        limit=63_400_000,
    )
    pieces = exchange(cut, "dp", DP)
    tab, mine, scale = call(
        tables_kernel,
        [((8, 512), I32), ((8, 384), I32), ((32, 128), F32)],
        [],
        dp,
        offsets,
        counts,
        adapter_slot,
        smem=4,
    )
    block = ((512, ROW), BF)
    (picked,) = call(pick_kernel, [block], [], tab, pieces)
    local = exchange(picked, "dp", DP)
    (mine,) = call(mark_kernel, [((8, 384), I32)], [], local, mine, output_gradient, any_in=1)
    tokens = (hidden, extra, mine)
    (partial,) = call(score_kernel, [((TP * SIG, 128), BF)], [], output_gradient, local, *tokens)
    signals = exchange(partial, "tensor", TP)
    (sums,) = call(sum_kernel, [block], [], output_gradient, signals, *tokens)
    gathered = exchange(sums, "dp", DP)
    (extra_gradient,) = call(extra_kernel, [((EXTRA, HID), BF)], [], signals, local, mine)
    back = lax.ppermute(extra_gradient, "dp", backward)
    head, tail = call(
        hidden_kernel,
        [((TOK, HID), BF), ((EXTRA, HID), BF)],
        [pltpu.VMEM((TOK - EXTRA, HID), BF), pltpu.SemaphoreType.DMA((4,))],
        signals,
        local,
        mine,
        hbm_out=1,
    )
    (slot_sums,) = call(
        reduce_kernel,
        [((256, LO), BF)],
        [pltpu.VMEM((256, LO), BF), pltpu.SemaphoreType.DMA((3,))],
        tab,
        gathered,
        hbm_out=1,
    )
    owned = exchange(slot_sums, "dp", DP)
    hidden_gradient, down_gradient, up_gradient = call(
        join_kernel,
        [((TOK, HID), BF), ((32, HID), F32), ((32, FEA), F32)],
        [
            pltpu.VMEM((32, HID), F32),
            pltpu.VMEM((32, FEA), F32),
            pltpu.VMEM((EXTRA, HID), BF),
            pltpu.SemaphoreType.DMA((9,)),
        ],
        head,
        scale,
        owned,
        tail,
        back,
        hbm_in=1,
        hbm_out=3,
        alias={0: 0},
    )
    return (
        hidden_gradient,
        down_gradient.reshape(2, RANK, HID),
        up_gradient.reshape(2, RANK, FEA),
    )


def solution(mesh):
    placed = (
        P("dp", "tensor"),
        P("dp", "tensor"),
        P("dp", None, "tensor"),
        P("dp", None, "tensor"),
        P(),
        P(),
        P(),
    )
    return jax.shard_map(
        on_device,
        mesh=mesh,
        in_specs=placed,
        out_specs=(P("dp", "tensor"), P("dp", None, "tensor"), P("dp", None, "tensor")),
        check_vma=False,
    )
```

```python
import jax
import jax.numpy as jnp
from jax import lax
from jax.experimental import pallas as pl
from jax.experimental.pallas import tpu as pltpu
from jax.sharding import PartitionSpec as P


adapter_factor = 2.0
BF = jnp.bfloat16
F32 = jnp.float32
I32 = jnp.int32
DP = 32
TP = 8
SLOTS = 64
RANK = 16
TOK = 256
HID = 3584
FEA = 1024
QH = HID // 4
QF = FEA // 4
ROW = QH + QF
LO = 640
HI = ROW - LO
EXTRA = 32
SIG = 72
LIMIT = 16 * 1024 * 1024


def iota(shape, axis):
    return lax.broadcasted_iota(I32, shape, axis)


def one_hot(condition):
    return jnp.where(condition, 1.0, 0.0).astype(BF)


def dot(a, b, ca=1, cb=0):
    return lax.dot_general(a, b, (((ca,), (cb,)), ((), ())), preferred_element_type=F32)


def travel_order(axis):
    i = iota((256, 256), 1 - axis)
    j = iota((256, 256), axis)
    rp, q, s, r, h = i >> 5, (i >> 3) & 3, (i >> 2) & 1, (i >> 1) & 1, i & 1
    return one_hot(j == q * 64 + h * 32 + s * 16 + rp * 2 + r)


def slot_hits(tab, shape, axis, part):
    c = iota(shape, axis)
    i = iota(shape, 1 - axis)
    hit = ((i >> 2).astype(F32) == tab) & (((i >> 1) & 1) == (c & 1)) & ((i & 1) == part)
    return one_hot(hit)


def tables_kernel(
    dp_ref, off_ref, cnt_ref, slot_ref, pick_ref, reduce_ref, order_ref, mine_ref, scale_ref
):
    dp = dp_ref[0]
    i = iota((8, 512), 1)
    first = (i >> 4) * TOK

    def count_before(a, low):
        return low + jnp.where(off_ref[a] + cnt_ref[a] <= first, 1, 0)

    wanted = lax.fori_loop(0, SLOTS, count_before, jnp.zeros((8, 512), I32), unroll=8)
    wanted += (i >> 1) & 7

    p = iota((8, 384), 1)
    own = p < TOK
    start = (dp - jnp.where(own, 0, 1)) * TOK
    at = start + jnp.where(own, p, p - EXTRA)

    def collect(a, carry):
        tab, mine, c0, c1 = carry
        off = off_ref[a]
        slot = slot_ref[a]
        hit = (wanted == a) & (off < first + TOK)
        tab = jnp.where(hit, slot, tab)
        mine = mine + jnp.where((off > start) & (off <= at), 1, 0)
        c0 = jnp.where(slot == 2 * dp, cnt_ref[a], c0)
        c1 = jnp.where(slot == 2 * dp + 1, cnt_ref[a], c1)
        return tab, mine, c0, c1

    init = (jnp.full((8, 512), -1, I32), jnp.zeros((8, 384), I32), jnp.int32(1), jnp.int32(1))
    tab, mine, c0, c1 = lax.fori_loop(0, SLOTS, collect, init, unroll=8)
    column = dot(tab.astype(F32).astype(BF), jnp.full((8, 256), 0.125, BF), 0, 0)
    row = tab[0:1, :].astype(F32)
    for part in range(2):
        pick_ref[part * 512 : (part + 1) * 512, :] = slot_hits(column, (512, 256), 0, part)
        reduce_ref[part * 256 : (part + 1) * 256, :] = slot_hits(row, (256, 512), 1, part)
    order_ref[...] = travel_order(0)
    extra = (p < TOK + EXTRA) & (mine == 8)
    mine_ref[...] = jnp.where(own, mine, jnp.where(extra, 0, -1))
    rows = iota((32, 128), 0)
    scale_ref[...] = adapter_factor / jnp.where(rows < 16, c0, c1).astype(F32)


def store_parts(value, out_ref, out_hbm, sems, first):
    copies = []
    for n, at in enumerate((0, 256, 512)):
        width = min(256, LO - at)
        out_ref[:, at : at + width] = value(slice(at, at + width)).astype(BF)
        lanes = pl.ds(at, width)
        copies.append(
            pltpu.make_async_copy(out_ref.at[:, lanes], out_hbm.at[:, lanes], sems.at[first + n])
        )
        copies[-1].start()
    for copy in copies:
        copy.wait()


def cut_kernel(down_hbm, up_hbm, out_hbm, down_ref, up_ref, out_ref, sems):
    copies = [
        pltpu.make_async_copy(down_hbm, down_ref, sems.at[0]),
        pltpu.make_async_copy(up_hbm, up_ref, sems.at[1]),
    ]
    for copy in copies:
        copy.start()
    order = travel_order(1)
    for copy in copies:
        copy.wait()
    parts = []
    for q in range(4):
        parts.append(down_ref[:, q * QH : q * QH + LO])
        parts.append(
            jnp.concatenate(
                [
                    down_ref[:, q * QH + LO : (q + 1) * QH],
                    up_ref[:, q * QF : (q + 1) * QF],
                    jnp.zeros((32, LO - HI), BF),
                ],
                axis=1,
            )
        )
    parts = jnp.concatenate(parts, axis=0)
    store_parts(lambda lanes: dot(order, parts[:, lanes]), out_ref, out_hbm, sems, 2)


def pick_kernel(hits_ref, in_ref, out_ref):
    out_ref[:, :LO] = dot(hits_ref[:512, :], in_ref[...]).astype(BF)
    out_ref[:, LO:] = dot(hits_ref[512:, :], in_ref[:, :HI]).astype(BF)


def quarter(ref, q, lanes):
    tiles = [ref[(rp * 4 + q) * 16 : (rp * 4 + q) * 16 + 16, lanes] for rp in range(8)]
    return jnp.concatenate(tiles, axis=0)


def members(mine_ref):
    k = (iota((128, TOK), 0) >> 1) & 7
    own = k == mine_ref[0:1, :TOK]
    k = (iota((128, EXTRA), 0) >> 1) & 7
    return own, k == mine_ref[0:1, TOK : TOK + EXTRA]


def rank_rows():
    o = iota((RANK, 128), 0)
    i = iota((RANK, 128), 1)
    return (i & 1) * 8 + (i >> 4) == o


def mark_kernel(in_hbm, mine_ref, grad_ref, out_ref):
    out_ref[...] = mine_ref[...]


def score_kernel(grad_ref, in_ref, hid_ref, extra_ref, mine_ref, out_ref):
    up = jnp.zeros((TOK + EXTRA, 128), F32)
    down = jnp.zeros((TOK + EXTRA, 128), F32)
    for q in range(4):
        lanes = slice(q * QH, (q + 1) * QH)
        tokens = jnp.concatenate([hid_ref[:, lanes], extra_ref[:, lanes]], axis=0)
        down += dot(tokens, quarter(in_ref, q, slice(0, QH)), 1, 1)
        lanes = slice(q * QF, (q + 1) * QF)
        behind = slice(HID + q * QF, HID + (q + 1) * QF)
        tokens = jnp.concatenate([grad_ref[:, lanes], extra_ref[:, behind]], axis=0)
        up += dot(tokens, quarter(in_ref, q, slice(QH, ROW)), 1, 1)
    mine = mine_ref[:, : TOK + EXTRA].astype(F32).astype(BF)
    mine = dot(mine, jnp.full((8, 128), 0.125, BF), 0, 0)
    member = ((iota((TOK + EXTRA, 128), 1) >> 1) & 7).astype(F32) == mine
    fold = jnp.where(rank_rows(), 1.0, 0.0)
    rows = jnp.concatenate(
        [
            lax.dot_general(
                fold,
                jnp.where(member, part, 0.0),
                (((1,), (1,)), ((), ())),
                preferred_element_type=F32,
                precision=lax.Precision.HIGHEST,
            )
            for part in (up, down)
        ],
        axis=0,
    )
    block = rows.astype(BF)
    tail = rows[:, TOK:]
    tail = jnp.concatenate([tail[i * 8 : i * 8 + 8, :] for i in range(4)], axis=1).astype(BF)
    for z in range(TP):
        out_ref[z * SIG : z * SIG + 32, :] = block[:, :128]
        out_ref[z * SIG + 32 : z * SIG + 64, :] = block[:, 128:TOK]
        out_ref[z * SIG + 64 : (z + 1) * SIG, :] = tail


def spread_signal(sig_ref, mine_ref, first):
    def total(at, rows):
        part = sig_ref[at : at + rows, :].astype(F32)
        for z in range(1, TP):
            part += sig_ref[z * SIG + at : z * SIG + at + rows, :].astype(F32)
        return part

    tail = total(64, 8)
    at = first * 4
    tail = jnp.concatenate(
        [tail[:, at : at + EXTRA], tail[:, at + EXTRA : at + 2 * EXTRA]], axis=0
    )
    parts = [total(first, RANK), total(32 + first, RANK)]
    own, extra = members(mine_ref)
    fold = one_hot(rank_rows())
    rows = dot(fold, jnp.concatenate(parts, axis=1).astype(BF), 0, 0)
    tail = dot(fold, tail.astype(BF), 0, 0)
    return jnp.where(own, rows, 0.0).astype(BF), jnp.where(extra, tail, 0.0).astype(BF)


def sum_kernel(grad_ref, sig_ref, hid_ref, extra_ref, mine_ref, out_ref):
    up = jnp.concatenate(spread_signal(sig_ref, mine_ref, 0), axis=1)
    down = jnp.concatenate(spread_signal(sig_ref, mine_ref, RANK), axis=1)
    for q in range(4):
        lanes = slice(q * QH, (q + 1) * QH)
        tokens = jnp.concatenate([hid_ref[:, lanes], extra_ref[:, lanes]], axis=0)
        sums = dot(up, tokens)
        for rp in range(8):
            at = (rp * 4 + q) * 16
            out_ref[at : at + 16, :QH] = sums[rp * 16 : rp * 16 + 16, :].astype(BF)
        lanes = slice(q * QF, (q + 1) * QF)
        behind = slice(HID + q * QF, HID + (q + 1) * QF)
        tokens = jnp.concatenate([grad_ref[:, lanes], extra_ref[:, behind]], axis=0)
        sums = dot(down, tokens)
        for rp in range(8):
            at = (rp * 4 + q) * 16
            out_ref[at : at + 16, QH:] = sums[rp * 16 : rp * 16 + 16, :].astype(BF)


def extra_kernel(sig_ref, in_ref, mine_ref, out_ref):
    _, up = spread_signal(sig_ref, mine_ref, 0)
    for q in range(4):
        out_ref[:, q * QH : (q + 1) * QH] = (
            adapter_factor * dot(up, quarter(in_ref, q, slice(0, QH)), 0, 0)
        ).astype(BF)


def hidden_kernel(sig_ref, in_ref, mine_ref, out_hbm, tail_ref, head_ref, sems):
    up, _ = spread_signal(sig_ref, mine_ref, 0)
    cut = TOK - EXTRA
    copies = []
    for q in range(4):
        lanes = slice(q * QH, (q + 1) * QH)
        rows = adapter_factor * dot(up, quarter(in_ref, q, slice(0, QH)), 0, 0)
        head_ref[:, lanes] = rows[:cut, :].astype(BF)
        tail_ref[:, lanes] = rows[cut:, :].astype(BF)
        copies.append(
            pltpu.make_async_copy(
                head_ref.at[:, pl.ds(q * QH, QH)],
                out_hbm.at[pl.ds(0, cut), pl.ds(q * QH, QH)],
                sems.at[q],
            )
        )
        copies[-1].start()
    for copy in copies:
        copy.wait()


def reduce_kernel(hits_ref, in_ref, out_hbm, out_ref, sems):
    def value(lanes):
        sums = dot(hits_ref[:256, :], in_ref[:, lanes])
        if lanes.start < HI:
            sums += dot(hits_ref[256:, :], in_ref[:, LO + lanes.start : LO + lanes.stop])
        return sums

    store_parts(value, out_ref, out_hbm, sems, 0)


def join_kernel(
    head_hbm,
    scale_ref,
    order_ref,
    in_ref,
    tail_ref,
    back_ref,
    hidden_hbm,
    down_hbm,
    up_hbm,
    down_ref,
    up_ref,
    rows_ref,
    sems,
):
    rows_ref[...] = (tail_ref[...].astype(F32) + back_ref[...].astype(F32)).astype(BF)
    copies = [
        pltpu.make_async_copy(
            rows_ref, hidden_hbm.at[pl.ds(TOK - EXTRA, EXTRA), :], sems.at[8]
        )
    ]
    copies[0].start()
    scale = scale_ref[:, 0:1]
    rows = dot(order_ref[...], in_ref[...])
    for q in range(4):
        low = rows[q * 64 : q * 64 + 32, :] * scale
        high = rows[q * 64 + 32 : q * 64 + 64, :] * scale
        down_ref[:, q * QH : q * QH + LO] = low
        down_ref[:, q * QH + LO : (q + 1) * QH] = high[:, : QH - LO]
        up_ref[:, q * QF : (q + 1) * QF] = high[:, QH - LO : HI]
        lanes = pl.ds(q * QH, QH)
        copies.append(
            pltpu.make_async_copy(down_ref.at[:, lanes], down_hbm.at[:, lanes], sems.at[q])
        )
        lanes = pl.ds(q * QF, QF)
        copies.append(pltpu.make_async_copy(up_ref.at[:, lanes], up_hbm.at[:, lanes], sems.at[4 + q]))
        for copy in copies[-2:]:
            copy.start()
    for copy in copies:
        copy.wait()


def call(kernel, outs, scratch, *args, smem=0, any_in=0, hbm_in=0, hbm_out=0, alias=None, limit=LIMIT):
    vmem = pl.BlockSpec(memory_space=pltpu.VMEM)
    scalar = pl.BlockSpec(memory_space=pltpu.SMEM)
    hbm = pl.BlockSpec(memory_space=pltpu.HBM)
    return pl.pallas_call(
        kernel,
        out_shape=[jax.ShapeDtypeStruct(s, t) for s, t in outs],
        in_specs=[scalar] * smem + [pl.BlockSpec(memory_space=pl.ANY)] * any_in
        + [hbm] * hbm_in
        + [vmem] * (len(args) - smem - any_in - hbm_in),
        out_specs=[hbm] * hbm_out + [vmem] * (len(outs) - hbm_out),
        scratch_shapes=scratch,
        input_output_aliases=alias or {},
        compiler_params=pltpu.CompilerParams(vmem_limit_bytes=limit),
    )(*args)


def exchange(x, axis, parts):
    block = x.reshape(parts, x.shape[0] // parts, x.shape[1])
    return lax.all_to_all(block, axis, 0, 0, tiled=True).reshape(x.shape)


def on_device(output_gradient, hidden, adapter_down, adapter_up, counts, offsets, adapter_slot):
    dp = lax.axis_index("dp").astype(I32).reshape(1)
    onward = [(i, i + 1) for i in range(DP - 1)]
    backward = [(i + 1, i) for i in range(DP - 1)]
    last = jnp.concatenate([hidden[TOK - EXTRA :], output_gradient[TOK - EXTRA :]], axis=1)
    extra = lax.ppermute(last, "dp", onward)
    down = adapter_down.reshape(2 * RANK, HID)
    up = adapter_up.reshape(2 * RANK, FEA)
    (cut,) = call(
        cut_kernel,
        [((256, LO), BF)],
        [
            pltpu.VMEM((32, HID), BF),
            pltpu.VMEM((32, FEA), BF),
            pltpu.VMEM((256, LO), BF),
            pltpu.SemaphoreType.DMA((5,)),
        ],
        down,
        up,
        hbm_in=2,
        hbm_out=1,
        limit=63_400_000,
    )
    pieces = exchange(cut, "dp", DP)
    pick_hits, reduce_hits, order, mine, scale = call(
        tables_kernel,
        [
            ((1024, 256), BF),
            ((512, 512), BF),
            ((256, 256), BF),
            ((8, 384), I32),
            ((32, 128), F32),
        ],
        [],
        dp,
        offsets,
        counts,
        adapter_slot,
        smem=4,
    )
    block = ((512, ROW), BF)
    (picked,) = call(pick_kernel, [block], [], pick_hits, pieces)
    local = exchange(picked, "dp", DP)
    (mine,) = call(mark_kernel, [((8, 384), I32)], [], local, mine, output_gradient, any_in=1)
    tokens = (hidden, extra, mine)
    (partial,) = call(score_kernel, [((TP * SIG, 128), BF)], [], output_gradient, local, *tokens)
    signals = exchange(partial, "tensor", TP)
    (sums,) = call(sum_kernel, [block], [], output_gradient, signals, *tokens)
    gathered = exchange(sums, "dp", DP)
    (extra_gradient,) = call(extra_kernel, [((EXTRA, HID), BF)], [], signals, local, mine)
    back = lax.ppermute(extra_gradient, "dp", backward)
    head, tail = call(
        hidden_kernel,
        [((TOK, HID), BF), ((EXTRA, HID), BF)],
        [pltpu.VMEM((TOK - EXTRA, HID), BF), pltpu.SemaphoreType.DMA((4,))],
        signals,
        local,
        mine,
        hbm_out=1,
    )
    (slot_sums,) = call(
        reduce_kernel,
        [((256, LO), BF)],
        [pltpu.VMEM((256, LO), BF), pltpu.SemaphoreType.DMA((3,))],
        reduce_hits,
        gathered,
        hbm_out=1,
    )
    owned = exchange(slot_sums, "dp", DP)
    hidden_gradient, down_gradient, up_gradient = call(
        join_kernel,
        [((TOK, HID), BF), ((32, HID), F32), ((32, FEA), F32)],
        [
            pltpu.VMEM((32, HID), F32),
            pltpu.VMEM((32, FEA), F32),
            pltpu.VMEM((EXTRA, HID), BF),
            pltpu.SemaphoreType.DMA((9,)),
        ],
        head,
        scale,
        order,
        owned,
        tail,
        back,
        hbm_in=1,
        hbm_out=3,
        alias={0: 0},
    )
    return (
        hidden_gradient,
        down_gradient.reshape(2, RANK, HID),
        up_gradient.reshape(2, RANK, FEA),
    )


def solution(mesh):
    placed = (
        P("dp", "tensor"),
        P("dp", "tensor"),
        P("dp", None, "tensor"),
        P("dp", None, "tensor"),
        P(),
        P(),
        P(),
    )
    return jax.shard_map(
        on_device,
        mesh=mesh,
        in_specs=placed,
        out_specs=(P("dp", "tensor"), P("dp", None, "tensor"), P("dp", None, "tensor")),
        check_vma=False,
    )
```

```python
import jax
import jax.numpy as jnp
from jax import lax
from jax.experimental import pallas as pl
from jax.experimental.pallas import tpu as pltpu
from jax.sharding import PartitionSpec as P


adapter_factor = 2.0
BF = jnp.bfloat16
F32 = jnp.float32
I32 = jnp.int32
DP = 32
TP = 8
SLOTS = 64
RANK = 16
TOK = 256
HID = 3584
FEA = 1024
QH = HID // 4
QF = FEA // 4
ROW = QH + QF
LO = 640
HI = ROW - LO
EXTRA = 32
SIG = 72
LIMIT = 16 * 1024 * 1024


def iota(shape, axis):
    return lax.broadcasted_iota(I32, shape, axis)


def one_hot(condition):
    return jnp.where(condition, 1.0, 0.0).astype(BF)


def dot(a, b, ca=1, cb=0):
    return lax.dot_general(a, b, (((ca,), (cb,)), ((), ())), preferred_element_type=F32)


def travel_order(axis):
    i = iota((256, 256), 1 - axis)
    j = iota((256, 256), axis)
    rp, q, s, r, h = i >> 5, (i >> 3) & 3, (i >> 2) & 1, (i >> 1) & 1, i & 1
    return one_hot(j == q * 64 + h * 32 + s * 16 + rp * 2 + r)


def slot_hits(tab, shape, axis, part):
    c = iota(shape, axis)
    i = iota(shape, 1 - axis)
    hit = ((i >> 2).astype(F32) == tab) & (((i >> 1) & 1) == (c & 1)) & ((i & 1) == part)
    return one_hot(hit)


def tables_kernel(
    dp_ref, off_ref, cnt_ref, slot_ref, pick_ref, reduce_ref, order_ref, mine_ref, scale_ref
):
    dp = dp_ref[0]
    i = iota((8, 512), 1)
    first = (i >> 4) * TOK

    def count_before(a, low):
        return low + jnp.where(off_ref[a] + cnt_ref[a] <= first, 1, 0)

    wanted = lax.fori_loop(0, SLOTS, count_before, jnp.zeros((8, 512), I32), unroll=8)
    wanted += (i >> 1) & 7

    p = iota((8, 384), 1)
    own = p < TOK
    start = (dp - jnp.where(own, 0, 1)) * TOK
    at = start + jnp.where(own, p, p - EXTRA)

    def collect(a, carry):
        tab, mine, c0, c1 = carry
        off = off_ref[a]
        slot = slot_ref[a]
        hit = (wanted == a) & (off < first + TOK)
        tab = jnp.where(hit, slot, tab)
        mine = mine + jnp.where((off > start) & (off <= at), 1, 0)
        c0 = jnp.where(slot == 2 * dp, cnt_ref[a], c0)
        c1 = jnp.where(slot == 2 * dp + 1, cnt_ref[a], c1)
        return tab, mine, c0, c1

    init = (jnp.full((8, 512), -1, I32), jnp.zeros((8, 384), I32), jnp.int32(1), jnp.int32(1))
    tab, mine, c0, c1 = lax.fori_loop(0, SLOTS, collect, init, unroll=8)
    column = dot(tab.astype(F32).astype(BF), jnp.full((8, 256), 0.125, BF), 0, 0)
    row = tab[0:1, :].astype(F32)
    for part in range(2):
        pick_ref[part * 512 : (part + 1) * 512, :] = slot_hits(column, (512, 256), 0, part)
        reduce_ref[part * 256 : (part + 1) * 256, :] = slot_hits(row, (256, 512), 1, part)
    order_ref[...] = travel_order(0)
    extra = (p < TOK + EXTRA) & (mine == 8)
    mine_ref[...] = jnp.where(own, mine, jnp.where(extra, 0, -1))
    rows = iota((32, 128), 0)
    scale_ref[...] = adapter_factor / jnp.where(rows < 16, c0, c1).astype(F32)


def store_parts(value, out_ref, out_hbm, sems, first):
    copies = []
    for n, at in enumerate((0, 256, 512)):
        width = min(256, LO - at)
        out_ref[:, at : at + width] = value(slice(at, at + width)).astype(BF)
        lanes = pl.ds(at, width)
        copies.append(
            pltpu.make_async_copy(out_ref.at[:, lanes], out_hbm.at[:, lanes], sems.at[first + n])
        )
        copies[-1].start()
    for copy in copies:
        copy.wait()


def cut_kernel(down_hbm, up_hbm, out_hbm, down_ref, up_ref, out_ref, sems):
    copies = [
        pltpu.make_async_copy(down_hbm, down_ref, sems.at[0]),
        pltpu.make_async_copy(up_hbm, up_ref, sems.at[1]),
    ]
    for copy in copies:
        copy.start()
    order = travel_order(1)
    for copy in copies:
        copy.wait()
    parts = []
    for q in range(4):
        parts.append(down_ref[:, q * QH : q * QH + LO])
        parts.append(
            jnp.concatenate(
                [
                    down_ref[:, q * QH + LO : (q + 1) * QH],
                    up_ref[:, q * QF : (q + 1) * QF],
                    jnp.zeros((32, LO - HI), BF),
                ],
                axis=1,
            )
        )
    parts = jnp.concatenate(parts, axis=0)
    store_parts(lambda lanes: dot(order, parts[:, lanes]), out_ref, out_hbm, sems, 2)


def pick_kernel(hits_ref, in_ref, out_ref):
    out_ref[:, :LO] = dot(hits_ref[:512, :], in_ref[...]).astype(BF)
    out_ref[:, LO:] = dot(hits_ref[512:, :], in_ref[:, :HI]).astype(BF)


def quarter(ref, q, lanes):
    tiles = [ref[(rp * 4 + q) * 16 : (rp * 4 + q) * 16 + 16, lanes] for rp in range(8)]
    return jnp.concatenate(tiles, axis=0)


def members(mine_ref):
    k = (iota((128, TOK), 0) >> 1) & 7
    own = k == mine_ref[0:1, :TOK]
    k = (iota((128, EXTRA), 0) >> 1) & 7
    return own, k == mine_ref[0:1, TOK : TOK + EXTRA]


def rank_rows():
    o = iota((RANK, 128), 0)
    i = iota((RANK, 128), 1)
    return (i & 1) * 8 + (i >> 4) == o


def mark_kernel(in_hbm, mine_ref, grad_ref, out_ref):
    out_ref[...] = mine_ref[...]


def score_kernel(grad_ref, in_ref, hid_ref, extra_ref, mine_ref, out_ref):
    up = jnp.zeros((TOK + EXTRA, 128), F32)
    down = jnp.zeros((TOK + EXTRA, 128), F32)
    for q in range(4):
        lanes = slice(q * QH, (q + 1) * QH)
        tokens = jnp.concatenate([hid_ref[:, lanes], extra_ref[:, lanes]], axis=0)
        down += dot(tokens, quarter(in_ref, q, slice(0, QH)), 1, 1)
        lanes = slice(q * QF, (q + 1) * QF)
        behind = slice(HID + q * QF, HID + (q + 1) * QF)
        tokens = jnp.concatenate([grad_ref[:, lanes], extra_ref[:, behind]], axis=0)
        up += dot(tokens, quarter(in_ref, q, slice(QH, ROW)), 1, 1)
    mine = mine_ref[:, : TOK + EXTRA].astype(F32).astype(BF)
    mine = dot(mine, jnp.full((8, 128), 0.125, BF), 0, 0)
    member = ((iota((TOK + EXTRA, 128), 1) >> 1) & 7).astype(F32) == mine
    fold = one_hot(rank_rows())
    rows = [dot(fold, jnp.where(member, part, 0.0).astype(BF), 1, 1) for part in (up, down)]
    rows = jnp.concatenate(rows, axis=0)
    block = rows.astype(BF)
    tail = rows[:, TOK:]
    tail = jnp.concatenate([tail[i * 8 : i * 8 + 8, :] for i in range(4)], axis=1).astype(BF)
    for z in range(TP):
        out_ref[z * SIG : z * SIG + 32, :] = block[:, :128]
        out_ref[z * SIG + 32 : z * SIG + 64, :] = block[:, 128:TOK]
        out_ref[z * SIG + 64 : (z + 1) * SIG, :] = tail


def spread_signal(sig_ref, mine_ref, first):
    def total(at, rows):
        part = sig_ref[at : at + rows, :].astype(F32)
        for z in range(1, TP):
            part += sig_ref[z * SIG + at : z * SIG + at + rows, :].astype(F32)
        return part

    tail = total(64, 8)
    at = first * 4
    tail = jnp.concatenate(
        [tail[:, at : at + EXTRA], tail[:, at + EXTRA : at + 2 * EXTRA]], axis=0
    )
    parts = [total(first, RANK), total(32 + first, RANK)]
    own, extra = members(mine_ref)
    fold = one_hot(rank_rows())
    rows = dot(fold, jnp.concatenate(parts, axis=1).astype(BF), 0, 0)
    tail = dot(fold, tail.astype(BF), 0, 0)
    return jnp.where(own, rows, 0.0).astype(BF), jnp.where(extra, tail, 0.0).astype(BF)


def sum_kernel(grad_ref, sig_ref, hid_ref, extra_ref, mine_ref, out_ref):
    for first, tokens_ref, lead, tiles, at_lane in (
        (0, hid_ref, 0, QH // 128, 0),
        (RANK, grad_ref, HID, QF // 128, QH),
    ):
        signal = jnp.concatenate(spread_signal(sig_ref, mine_ref, first), axis=1)
        for n in range(tokens_ref.shape[1] // 256):
            lanes = slice(n * 256, (n + 1) * 256)
            behind = slice(lead + n * 256, lead + (n + 1) * 256)
            tokens = jnp.concatenate([tokens_ref[:, lanes], extra_ref[:, behind]], axis=0)
            sums = dot(signal, tokens)
            for half in range(2):
                q, tile = divmod(2 * n + half, tiles)
                part = sums[:, half * 128 : (half + 1) * 128]
                lane = at_lane + tile * 128
                for rp in range(8):
                    at = (rp * 4 + q) * 16
                    out_ref[at : at + 16, lane : lane + 128] = part[
                        rp * 16 : rp * 16 + 16, :
                    ].astype(BF)


def extra_kernel(sig_ref, in_ref, mine_ref, out_ref):
    _, up = spread_signal(sig_ref, mine_ref, 0)
    for q in range(4):
        out_ref[:, q * QH : (q + 1) * QH] = (
            adapter_factor * dot(up, quarter(in_ref, q, slice(0, QH)), 0, 0)
        ).astype(BF)


def hidden_kernel(sig_ref, in_ref, mine_ref, out_hbm, tail_ref, head_ref, sems):
    up, _ = spread_signal(sig_ref, mine_ref, 0)
    cut = TOK - EXTRA
    copies = []
    for q in range(4):
        lanes = slice(q * QH, (q + 1) * QH)
        rows = adapter_factor * dot(up, quarter(in_ref, q, slice(0, QH)), 0, 0)
        head_ref[:, lanes] = rows[:cut, :].astype(BF)
        tail_ref[:, lanes] = rows[cut:, :].astype(BF)
        copies.append(
            pltpu.make_async_copy(
                head_ref.at[:, pl.ds(q * QH, QH)],
                out_hbm.at[pl.ds(0, cut), pl.ds(q * QH, QH)],
                sems.at[q],
            )
        )
        copies[-1].start()
    for copy in copies:
        copy.wait()


def reduce_kernel(hits_ref, in_ref, out_hbm, out_ref, sems):
    def value(lanes):
        sums = dot(hits_ref[:256, :], in_ref[:, lanes])
        if lanes.start < HI:
            sums += dot(hits_ref[256:, :], in_ref[:, LO + lanes.start : LO + lanes.stop])
        return sums

    store_parts(value, out_ref, out_hbm, sems, 0)


def join_kernel(
    head_hbm,
    scale_ref,
    order_ref,
    in_ref,
    tail_ref,
    back_ref,
    hidden_hbm,
    down_hbm,
    up_hbm,
    down_ref,
    up_ref,
    rows_ref,
    sems,
):
    rows_ref[...] = (tail_ref[...].astype(F32) + back_ref[...].astype(F32)).astype(BF)
    copies = [
        pltpu.make_async_copy(
            rows_ref, hidden_hbm.at[pl.ds(TOK - EXTRA, EXTRA), :], sems.at[8]
        )
    ]
    copies[0].start()
    scale = scale_ref[:, 0:1]
    rows = dot(order_ref[...], in_ref[...])
    for q in range(4):
        low = rows[q * 64 : q * 64 + 32, :] * scale
        high = rows[q * 64 + 32 : q * 64 + 64, :] * scale
        down_ref[:, q * QH : q * QH + LO] = low
        down_ref[:, q * QH + LO : (q + 1) * QH] = high[:, : QH - LO]
        up_ref[:, q * QF : (q + 1) * QF] = high[:, QH - LO : HI]
        lanes = pl.ds(q * QH, QH)
        copies.append(
            pltpu.make_async_copy(down_ref.at[:, lanes], down_hbm.at[:, lanes], sems.at[q])
        )
        lanes = pl.ds(q * QF, QF)
        copies.append(pltpu.make_async_copy(up_ref.at[:, lanes], up_hbm.at[:, lanes], sems.at[4 + q]))
        for copy in copies[-2:]:
            copy.start()
    for copy in copies:
        copy.wait()


def call(kernel, outs, scratch, *args, smem=0, any_in=0, hbm_in=0, hbm_out=0, alias=None, limit=LIMIT):
    vmem = pl.BlockSpec(memory_space=pltpu.VMEM)
    scalar = pl.BlockSpec(memory_space=pltpu.SMEM)
    hbm = pl.BlockSpec(memory_space=pltpu.HBM)
    return pl.pallas_call(
        kernel,
        out_shape=[jax.ShapeDtypeStruct(s, t) for s, t in outs],
        in_specs=[scalar] * smem + [pl.BlockSpec(memory_space=pl.ANY)] * any_in
        + [hbm] * hbm_in
        + [vmem] * (len(args) - smem - any_in - hbm_in),
        out_specs=[hbm] * hbm_out + [vmem] * (len(outs) - hbm_out),
        scratch_shapes=scratch,
        input_output_aliases=alias or {},
        compiler_params=pltpu.CompilerParams(vmem_limit_bytes=limit),
    )(*args)


def exchange(x, axis, parts):
    block = x.reshape(parts, x.shape[0] // parts, x.shape[1])
    return lax.all_to_all(block, axis, 0, 0, tiled=True).reshape(x.shape)


def on_device(output_gradient, hidden, adapter_down, adapter_up, counts, offsets, adapter_slot):
    dp = lax.axis_index("dp").astype(I32).reshape(1)
    onward = [(i, i + 1) for i in range(DP - 1)]
    backward = [(i + 1, i) for i in range(DP - 1)]
    last = jnp.concatenate([hidden[TOK - EXTRA :], output_gradient[TOK - EXTRA :]], axis=1)
    extra = lax.ppermute(last, "dp", onward)
    down = adapter_down.reshape(2 * RANK, HID)
    up = adapter_up.reshape(2 * RANK, FEA)
    (cut,) = call(
        cut_kernel,
        [((256, LO), BF)],
        [
            pltpu.VMEM((32, HID), BF),
            pltpu.VMEM((32, FEA), BF),
            pltpu.VMEM((256, LO), BF),
            pltpu.SemaphoreType.DMA((5,)),
        ],
        down,
        up,
        hbm_in=2,
        hbm_out=1,
        limit=63_400_000,
    )
    pieces = exchange(cut, "dp", DP)
    pick_hits, reduce_hits, order, mine, scale = call(
        tables_kernel,
        [
            ((1024, 256), BF),
            ((512, 512), BF),
            ((256, 256), BF),
            ((8, 384), I32),
            ((32, 128), F32),
        ],
        [],
        dp,
        offsets,
        counts,
        adapter_slot,
        smem=4,
    )
    block = ((512, ROW), BF)
    (picked,) = call(pick_kernel, [block], [], pick_hits, pieces)
    local = exchange(picked, "dp", DP)
    (mine,) = call(mark_kernel, [((8, 384), I32)], [], local, mine, output_gradient, any_in=1)
    tokens = (hidden, extra, mine)
    (partial,) = call(score_kernel, [((TP * SIG, 128), BF)], [], output_gradient, local, *tokens)
    signals = exchange(partial, "tensor", TP)
    (sums,) = call(sum_kernel, [block], [], output_gradient, signals, *tokens)
    gathered = exchange(sums, "dp", DP)
    (extra_gradient,) = call(extra_kernel, [((EXTRA, HID), BF)], [], signals, local, mine)
    back = lax.ppermute(extra_gradient, "dp", backward)
    head, tail = call(
        hidden_kernel,
        [((TOK, HID), BF), ((EXTRA, HID), BF)],
        [pltpu.VMEM((TOK - EXTRA, HID), BF), pltpu.SemaphoreType.DMA((4,))],
        signals,
        local,
        mine,
        hbm_out=1,
    )
    (slot_sums,) = call(
        reduce_kernel,
        [((256, LO), BF)],
        [pltpu.VMEM((256, LO), BF), pltpu.SemaphoreType.DMA((3,))],
        reduce_hits,
        gathered,
        hbm_out=1,
    )
    owned = exchange(slot_sums, "dp", DP)
    hidden_gradient, down_gradient, up_gradient = call(
        join_kernel,
        [((TOK, HID), BF), ((32, HID), F32), ((32, FEA), F32)],
        [
            pltpu.VMEM((32, HID), F32),
            pltpu.VMEM((32, FEA), F32),
            pltpu.VMEM((EXTRA, HID), BF),
            pltpu.SemaphoreType.DMA((9,)),
        ],
        head,
        scale,
        order,
        owned,
        tail,
        back,
        hbm_in=1,
        hbm_out=3,
        alias={0: 0},
    )
    return (
        hidden_gradient,
        down_gradient.reshape(2, RANK, HID),
        up_gradient.reshape(2, RANK, FEA),
    )


def solution(mesh):
    placed = (
        P("dp", "tensor"),
        P("dp", "tensor"),
        P("dp", None, "tensor"),
        P("dp", None, "tensor"),
        P(),
        P(),
        P(),
    )
    return jax.shard_map(
        on_device,
        mesh=mesh,
        in_specs=placed,
        out_specs=(P("dp", "tensor"), P("dp", None, "tensor"), P("dp", None, "tensor")),
        check_vma=False,
    )
```

```python
import jax
import jax.numpy as jnp
from jax import lax
from jax.experimental import pallas as pl
from jax.experimental.pallas import tpu as pltpu
from jax.sharding import PartitionSpec as P


adapter_factor = 2.0
BF = jnp.bfloat16
F32 = jnp.float32
I32 = jnp.int32
DP = 32
TP = 8
SLOTS = 64
RANK = 16
TOK = 256
HID = 3584
FEA = 1024
QH = HID // 4
QF = FEA // 4
ROW = QH + QF
LO = 640
HI = ROW - LO
EXTRA = 32
SIG = 72
LIMIT = 16 * 1024 * 1024


def iota(shape, axis):
    return lax.broadcasted_iota(I32, shape, axis)


def one_hot(condition):
    return jnp.where(condition, 1.0, 0.0).astype(BF)


def dot(a, b, ca=1, cb=0):
    return lax.dot_general(a, b, (((ca,), (cb,)), ((), ())), preferred_element_type=F32)


def travel_order(axis):
    i = iota((256, 256), 1 - axis)
    j = iota((256, 256), axis)
    rp, q, s, r, h = i >> 5, (i >> 3) & 3, (i >> 2) & 1, (i >> 1) & 1, i & 1
    return one_hot(j == q * 64 + h * 32 + s * 16 + rp * 2 + r)


def slot_hits(tab, shape, axis, part):
    c = iota(shape, axis)
    i = iota(shape, 1 - axis)
    hit = ((i >> 2).astype(F32) == tab) & (((i >> 1) & 1) == (c & 1)) & ((i & 1) == part)
    return one_hot(hit)


def tables_kernel(
    dp_ref, off_ref, cnt_ref, slot_ref, pick_ref, reduce_ref, order_ref, mine_ref, scale_ref
):
    dp = dp_ref[0]
    i = iota((8, 512), 1)
    first = (i >> 4) * TOK

    def count_before(a, low):
        return low + jnp.where(off_ref[a] + cnt_ref[a] <= first, 1, 0)

    wanted = lax.fori_loop(0, SLOTS, count_before, jnp.zeros((8, 512), I32), unroll=8)
    wanted += (i >> 1) & 7

    p = iota((8, 384), 1)
    own = p < TOK
    start = (dp - jnp.where(own, 0, 1)) * TOK
    at = start + jnp.where(own, p, p - EXTRA)

    def collect(a, carry):
        tab, mine, c0, c1 = carry
        off = off_ref[a]
        slot = slot_ref[a]
        hit = (wanted == a) & (off < first + TOK)
        tab = jnp.where(hit, slot, tab)
        mine = mine + jnp.where((off > start) & (off <= at), 1, 0)
        c0 = jnp.where(slot == 2 * dp, cnt_ref[a], c0)
        c1 = jnp.where(slot == 2 * dp + 1, cnt_ref[a], c1)
        return tab, mine, c0, c1

    init = (jnp.full((8, 512), -1, I32), jnp.zeros((8, 384), I32), jnp.int32(1), jnp.int32(1))
    tab, mine, c0, c1 = lax.fori_loop(0, SLOTS, collect, init, unroll=8)
    column = dot(tab.astype(F32).astype(BF), jnp.full((8, 256), 0.125, BF), 0, 0)
    row = tab[0:1, :].astype(F32)
    for part in range(2):
        pick_ref[part * 512 : (part + 1) * 512, :] = slot_hits(column, (512, 256), 0, part)
        reduce_ref[part * 256 : (part + 1) * 256, :] = slot_hits(row, (256, 512), 1, part)
    order_ref[...] = travel_order(0)
    extra = (p < TOK + EXTRA) & (mine == 8)
    mine_ref[...] = jnp.where(own, mine, jnp.where(extra, 0, -1))
    rows = iota((32, 128), 0)
    scale_ref[...] = adapter_factor / jnp.where(rows < 16, c0, c1).astype(F32)


def store_parts(value, out_ref, out_hbm, sems, first):
    copies = []
    for n, at in enumerate((0, 256, 512)):
        width = min(256, LO - at)
        out_ref[:, at : at + width] = value(slice(at, at + width)).astype(BF)
        lanes = pl.ds(at, width)
        copies.append(
            pltpu.make_async_copy(out_ref.at[:, lanes], out_hbm.at[:, lanes], sems.at[first + n])
        )
        copies[-1].start()
    for copy in copies:
        copy.wait()


def cut_kernel(down_hbm, up_hbm, out_hbm, down_ref, up_ref, out_ref, sems):
    copies = [
        pltpu.make_async_copy(down_hbm, down_ref, sems.at[0]),
        pltpu.make_async_copy(up_hbm, up_ref, sems.at[1]),
    ]
    for copy in copies:
        copy.start()
    order = travel_order(1)
    for copy in copies:
        copy.wait()
    parts = []
    for q in range(4):
        parts.append(down_ref[:, q * QH : q * QH + LO])
        parts.append(
            jnp.concatenate(
                [
                    down_ref[:, q * QH + LO : (q + 1) * QH],
                    up_ref[:, q * QF : (q + 1) * QF],
                    jnp.zeros((32, LO - HI), BF),
                ],
                axis=1,
            )
        )
    parts = jnp.concatenate(parts, axis=0)
    store_parts(lambda lanes: dot(order, parts[:, lanes]), out_ref, out_hbm, sems, 2)


def pick_kernel(hits_ref, in_ref, out_ref):
    out_ref[:, :LO] = dot(hits_ref[:512, :], in_ref[...]).astype(BF)
    out_ref[:, LO:] = dot(hits_ref[512:, :], in_ref[:, :HI]).astype(BF)


def quarter(ref, q, lanes):
    tiles = [ref[(rp * 4 + q) * 16 : (rp * 4 + q) * 16 + 16, lanes] for rp in range(8)]
    return jnp.concatenate(tiles, axis=0)


def members(mine_ref):
    k = (iota((128, TOK), 0) >> 1) & 7
    own = k == mine_ref[0:1, :TOK]
    k = (iota((128, EXTRA), 0) >> 1) & 7
    return own, k == mine_ref[0:1, TOK : TOK + EXTRA]


def rank_rows():
    o = iota((RANK, 128), 0)
    i = iota((RANK, 128), 1)
    return (i & 1) * 8 + (i >> 4) == o


def mark_kernel(in_hbm, mine_ref, grad_ref, out_ref):
    out_ref[...] = mine_ref[...]


def score_kernel(grad_ref, in_ref, hid_ref, extra_ref, mine_ref, out_ref):
    up = jnp.zeros((TOK + EXTRA, 128), F32)
    down = jnp.zeros((TOK + EXTRA, 128), F32)
    for q in range(4):
        lanes = slice(q * QH, (q + 1) * QH)
        tokens = jnp.concatenate([hid_ref[:, lanes], extra_ref[:, lanes]], axis=0)
        down += dot(tokens, quarter(in_ref, q, slice(0, QH)), 1, 1)
        lanes = slice(q * QF, (q + 1) * QF)
        behind = slice(HID + q * QF, HID + (q + 1) * QF)
        tokens = jnp.concatenate([grad_ref[:, lanes], extra_ref[:, behind]], axis=0)
        up += dot(tokens, quarter(in_ref, q, slice(QH, ROW)), 1, 1)
    mine = mine_ref[:, : TOK + EXTRA].astype(F32).astype(BF)
    mine = dot(mine, jnp.full((8, 128), 0.125, BF), 0, 0)
    member = ((iota((TOK + EXTRA, 128), 1) >> 1) & 7).astype(F32) == mine
    fold = one_hot(rank_rows())
    rows = [dot(fold, jnp.where(member, part, 0.0).astype(BF), 1, 1) for part in (up, down)]
    rows = jnp.concatenate(rows, axis=0)
    block = rows.astype(BF)
    tail = rows[:, TOK:]
    tail = jnp.concatenate([tail[i * 8 : i * 8 + 8, :] for i in range(4)], axis=1).astype(BF)
    for z in range(TP):
        out_ref[z * SIG : z * SIG + 32, :] = block[:, :128]
        out_ref[z * SIG + 32 : z * SIG + 64, :] = block[:, 128:TOK]
        out_ref[z * SIG + 64 : (z + 1) * SIG, :] = tail


def spread_signal(sig_ref, mine_ref, first):
    def total(at, rows):
        part = sig_ref[at : at + rows, :].astype(F32)
        for z in range(1, TP):
            part += sig_ref[z * SIG + at : z * SIG + at + rows, :].astype(F32)
        return part

    tail = total(64, 8)
    at = first * 4
    tail = jnp.concatenate(
        [tail[:, at : at + EXTRA], tail[:, at + EXTRA : at + 2 * EXTRA]], axis=0
    )
    parts = [total(first, RANK), total(32 + first, RANK)]
    own, extra = members(mine_ref)
    fold = one_hot(rank_rows())
    rows = dot(fold, jnp.concatenate(parts, axis=1).astype(BF), 0, 0)
    tail = dot(fold, tail.astype(BF), 0, 0)
    return jnp.where(own, rows, 0.0).astype(BF), jnp.where(extra, tail, 0.0).astype(BF)


def sum_kernel(grad_ref, sig_ref, hid_ref, extra_ref, mine_ref, out_hbm, out_ref, sems):
    up = jnp.concatenate(spread_signal(sig_ref, mine_ref, 0), axis=1)
    down = jnp.concatenate(spread_signal(sig_ref, mine_ref, RANK), axis=1)
    copies = []
    for q in range(4):
        lanes = slice(q * QH, (q + 1) * QH)
        tokens = jnp.concatenate([hid_ref[:, lanes], extra_ref[:, lanes]], axis=0)
        sums = dot(up, tokens)
        rows = slice(q * 16, q * 16 + 16)
        for rp in range(8):
            out_ref[rp, rows, :QH] = sums[rp * 16 : rp * 16 + 16, :].astype(BF)
        lanes = slice(q * QF, (q + 1) * QF)
        behind = slice(HID + q * QF, HID + (q + 1) * QF)
        tokens = jnp.concatenate([grad_ref[:, lanes], extra_ref[:, behind]], axis=0)
        sums = dot(down, tokens)
        for rp in range(8):
            out_ref[rp, rows, QH:] = sums[rp * 16 : rp * 16 + 16, :].astype(BF)
        rows = pl.ds(q * 16, 16)
        copies.append(
            pltpu.make_async_copy(out_ref.at[:, rows, :], out_hbm.at[:, rows, :], sems.at[q])
        )
        copies[-1].start()
    for copy in copies:
        copy.wait()


def extra_kernel(sig_ref, in_ref, mine_ref, out_ref):
    _, up = spread_signal(sig_ref, mine_ref, 0)
    for q in range(4):
        out_ref[:, q * QH : (q + 1) * QH] = (
            adapter_factor * dot(up, quarter(in_ref, q, slice(0, QH)), 0, 0)
        ).astype(BF)


def hidden_kernel(sig_ref, in_ref, mine_ref, out_hbm, tail_ref, head_ref, sems):
    up, _ = spread_signal(sig_ref, mine_ref, 0)
    cut = TOK - EXTRA
    copies = []
    for q in range(4):
        lanes = slice(q * QH, (q + 1) * QH)
        rows = adapter_factor * dot(up, quarter(in_ref, q, slice(0, QH)), 0, 0)
        head_ref[:, lanes] = rows[:cut, :].astype(BF)
        tail_ref[:, lanes] = rows[cut:, :].astype(BF)
        copies.append(
            pltpu.make_async_copy(
                head_ref.at[:, pl.ds(q * QH, QH)],
                out_hbm.at[pl.ds(0, cut), pl.ds(q * QH, QH)],
                sems.at[q],
            )
        )
        copies[-1].start()
    for copy in copies:
        copy.wait()


def reduce_kernel(after_hbm, hits_ref, in_ref, out_ref):
    low = dot(hits_ref[:256, :], in_ref[:, :LO])
    high = dot(hits_ref[256:, :], in_ref[:, LO:])
    out_ref[:, :HI] = (low[:, :HI] + high).astype(BF)
    out_ref[:, HI:] = low[:, HI:].astype(BF)


def join_kernel(
    head_hbm,
    scale_ref,
    order_ref,
    in_ref,
    tail_ref,
    back_ref,
    hidden_hbm,
    down_hbm,
    up_hbm,
    down_ref,
    up_ref,
    rows_ref,
    sems,
):
    rows_ref[...] = (tail_ref[...].astype(F32) + back_ref[...].astype(F32)).astype(BF)
    copies = [
        pltpu.make_async_copy(
            rows_ref, hidden_hbm.at[pl.ds(TOK - EXTRA, EXTRA), :], sems.at[8]
        )
    ]
    copies[0].start()
    scale = scale_ref[:, 0:1]
    rows = dot(order_ref[...], in_ref[...])
    for q in range(4):
        low = rows[q * 64 : q * 64 + 32, :] * scale
        high = rows[q * 64 + 32 : q * 64 + 64, :] * scale
        down_ref[:, q * QH : q * QH + LO] = low
        down_ref[:, q * QH + LO : (q + 1) * QH] = high[:, : QH - LO]
        up_ref[:, q * QF : (q + 1) * QF] = high[:, QH - LO : HI]
        lanes = pl.ds(q * QH, QH)
        copies.append(
            pltpu.make_async_copy(down_ref.at[:, lanes], down_hbm.at[:, lanes], sems.at[q])
        )
        lanes = pl.ds(q * QF, QF)
        copies.append(pltpu.make_async_copy(up_ref.at[:, lanes], up_hbm.at[:, lanes], sems.at[4 + q]))
        for copy in copies[-2:]:
            copy.start()
    for copy in copies:
        copy.wait()


def call(kernel, outs, scratch, *args, smem=0, any_in=0, hbm_in=0, hbm_out=0, alias=None, limit=LIMIT):
    vmem = pl.BlockSpec(memory_space=pltpu.VMEM)
    scalar = pl.BlockSpec(memory_space=pltpu.SMEM)
    hbm = pl.BlockSpec(memory_space=pltpu.HBM)
    return pl.pallas_call(
        kernel,
        out_shape=[jax.ShapeDtypeStruct(s, t) for s, t in outs],
        in_specs=[scalar] * smem + [pl.BlockSpec(memory_space=pl.ANY)] * any_in
        + [hbm] * hbm_in
        + [vmem] * (len(args) - smem - any_in - hbm_in),
        out_specs=[hbm] * hbm_out + [vmem] * (len(outs) - hbm_out),
        scratch_shapes=scratch,
        input_output_aliases=alias or {},
        compiler_params=pltpu.CompilerParams(vmem_limit_bytes=limit),
    )(*args)


def exchange(x, axis, parts):
    block = x.reshape(parts, x.shape[0] // parts, x.shape[1])
    return lax.all_to_all(block, axis, 0, 0, tiled=True).reshape(x.shape)


def on_device(output_gradient, hidden, adapter_down, adapter_up, counts, offsets, adapter_slot):
    dp = lax.axis_index("dp").astype(I32).reshape(1)
    onward = [(i, i + 1) for i in range(DP - 1)]
    backward = [(i + 1, i) for i in range(DP - 1)]
    last = jnp.concatenate([hidden[TOK - EXTRA :], output_gradient[TOK - EXTRA :]], axis=1)
    extra = lax.ppermute(last, "dp", onward)
    down = adapter_down.reshape(2 * RANK, HID)
    up = adapter_up.reshape(2 * RANK, FEA)
    (cut,) = call(
        cut_kernel,
        [((256, LO), BF)],
        [
            pltpu.VMEM((32, HID), BF),
            pltpu.VMEM((32, FEA), BF),
            pltpu.VMEM((256, LO), BF),
            pltpu.SemaphoreType.DMA((5,)),
        ],
        down,
        up,
        hbm_in=2,
        hbm_out=1,
        limit=63_400_000,
    )
    pieces = exchange(cut, "dp", DP)
    pick_hits, reduce_hits, order, mine, scale = call(
        tables_kernel,
        [
            ((1024, 256), BF),
            ((512, 512), BF),
            ((256, 256), BF),
            ((8, 384), I32),
            ((32, 128), F32),
        ],
        [],
        dp,
        offsets,
        counts,
        adapter_slot,
        smem=4,
    )
    block = ((512, ROW), BF)
    (picked,) = call(pick_kernel, [block], [], pick_hits, pieces)
    local = exchange(picked, "dp", DP)
    (mine,) = call(mark_kernel, [((8, 384), I32)], [], local, mine, output_gradient, any_in=1)
    tokens = (hidden, extra, mine)
    (partial,) = call(score_kernel, [((TP * SIG, 128), BF)], [], output_gradient, local, *tokens)
    signals = exchange(partial, "tensor", TP)
    (sums,) = call(
        sum_kernel,
        [((8, 64, ROW), BF)],
        [pltpu.VMEM((8, 64, ROW), BF), pltpu.SemaphoreType.DMA((4,))],
        output_gradient,
        signals,
        *tokens,
        hbm_out=1,
    )
    sums = sums.reshape(512, ROW)
    gathered = exchange(sums, "dp", DP)
    (extra_gradient,) = call(extra_kernel, [((EXTRA, HID), BF)], [], signals, local, mine)
    back = lax.ppermute(extra_gradient, "dp", backward)
    head, tail = call(
        hidden_kernel,
        [((TOK, HID), BF), ((EXTRA, HID), BF)],
        [pltpu.VMEM((TOK - EXTRA, HID), BF), pltpu.SemaphoreType.DMA((4,))],
        signals,
        local,
        mine,
        hbm_out=1,
    )
    (slot_sums,) = call(reduce_kernel, [((256, LO), BF)], [], back, reduce_hits, gathered, any_in=1)
    owned = exchange(slot_sums, "dp", DP)
    hidden_gradient, down_gradient, up_gradient = call(
        join_kernel,
        [((TOK, HID), BF), ((32, HID), F32), ((32, FEA), F32)],
        [
            pltpu.VMEM((32, HID), F32),
            pltpu.VMEM((32, FEA), F32),
            pltpu.VMEM((EXTRA, HID), BF),
            pltpu.SemaphoreType.DMA((9,)),
        ],
        head,
        scale,
        order,
        owned,
        tail,
        back,
        hbm_in=1,
        hbm_out=3,
        alias={0: 0},
    )
    return (
        hidden_gradient,
        down_gradient.reshape(2, RANK, HID),
        up_gradient.reshape(2, RANK, FEA),
    )


def solution(mesh):
    placed = (
        P("dp", "tensor"),
        P("dp", "tensor"),
        P("dp", None, "tensor"),
        P("dp", None, "tensor"),
        P(),
        P(),
        P(),
    )
    return jax.shard_map(
        on_device,
        mesh=mesh,
        in_specs=placed,
        out_specs=(P("dp", "tensor"), P("dp", None, "tensor"), P("dp", None, "tensor")),
        check_vma=False,
    )
```

```python
import jax
import jax.numpy as jnp
from jax import lax
from jax.experimental import pallas as pl
from jax.experimental.pallas import tpu as pltpu
from jax.sharding import PartitionSpec as P


adapter_factor = 2.0
BF = jnp.bfloat16
F32 = jnp.float32
I32 = jnp.int32
DP = 32
TP = 8
SLOTS = 64
RANK = 16
TOK = 256
HID = 3584
FEA = 1024
QH = HID // 4
QF = FEA // 4
ROW = QH + QF
LO = 640
HI = ROW - LO
EXTRA = 32
SIG = 72
LIMIT = 16 * 1024 * 1024


def iota(shape, axis):
    return lax.broadcasted_iota(I32, shape, axis)


def one_hot(condition):
    return jnp.where(condition, 1.0, 0.0).astype(BF)


def dot(a, b, ca=1, cb=0):
    return lax.dot_general(a, b, (((ca,), (cb,)), ((), ())), preferred_element_type=F32)


def travel_order(axis):
    i = iota((256, 256), 1 - axis)
    j = iota((256, 256), axis)
    rp, q, s, r, h = i >> 5, (i >> 3) & 3, (i >> 2) & 1, (i >> 1) & 1, i & 1
    return one_hot(j == q * 64 + h * 32 + s * 16 + rp * 2 + r)


def slot_hits(tab, shape, axis, part):
    c = iota(shape, axis)
    i = iota(shape, 1 - axis)
    hit = ((i >> 2).astype(F32) == tab) & (((i >> 1) & 1) == (c & 1)) & ((i & 1) == part)
    return one_hot(hit)


def tables_kernel(
    dp_ref, off_ref, cnt_ref, slot_ref, pick_ref, reduce_ref, order_ref, mine_ref, scale_ref
):
    dp = dp_ref[0]
    i = iota((8, 512), 1)
    first = (i >> 4) * TOK

    def count_before(a, low):
        return low + jnp.where(off_ref[a] + cnt_ref[a] <= first, 1, 0)

    wanted = lax.fori_loop(0, SLOTS, count_before, jnp.zeros((8, 512), I32), unroll=8)
    wanted += (i >> 1) & 7

    p = iota((8, 384), 1)
    own = p < TOK
    start = (dp - jnp.where(own, 0, 1)) * TOK
    at = start + jnp.where(own, p, p - EXTRA)

    def collect(a, carry):
        tab, mine, c0, c1 = carry
        off = off_ref[a]
        slot = slot_ref[a]
        hit = (wanted == a) & (off < first + TOK)
        tab = jnp.where(hit, slot, tab)
        mine = mine + jnp.where((off > start) & (off <= at), 1, 0)
        c0 = jnp.where(slot == 2 * dp, cnt_ref[a], c0)
        c1 = jnp.where(slot == 2 * dp + 1, cnt_ref[a], c1)
        return tab, mine, c0, c1

    init = (jnp.full((8, 512), -1, I32), jnp.zeros((8, 384), I32), jnp.int32(1), jnp.int32(1))
    tab, mine, c0, c1 = lax.fori_loop(0, SLOTS, collect, init, unroll=8)
    column = dot(tab.astype(F32).astype(BF), jnp.full((8, 256), 0.125, BF), 0, 0)
    row = tab[0:1, :].astype(F32)
    for part in range(2):
        pick_ref[part * 512 : (part + 1) * 512, :] = slot_hits(column, (512, 256), 0, part)
        reduce_ref[part * 256 : (part + 1) * 256, :] = slot_hits(row, (256, 512), 1, part)
    order_ref[...] = travel_order(0)
    extra = (p < TOK + EXTRA) & (mine == 8)
    mine_ref[...] = jnp.where(own, mine, jnp.where(extra, 0, -1))
    rows = iota((32, 128), 0)
    scale_ref[...] = adapter_factor / jnp.where(rows < 16, c0, c1).astype(F32)


def store_parts(value, out_ref, out_hbm, sems, first):
    copies = []
    for n, at in enumerate((0, 256, 512)):
        width = min(256, LO - at)
        out_ref[:, at : at + width] = value(slice(at, at + width)).astype(BF)
        lanes = pl.ds(at, width)
        copies.append(
            pltpu.make_async_copy(out_ref.at[:, lanes], out_hbm.at[:, lanes], sems.at[first + n])
        )
        copies[-1].start()
    for copy in copies:
        copy.wait()


def cut_kernel(down_hbm, up_hbm, out_hbm, down_ref, up_ref, out_ref, sems):
    copies = [
        pltpu.make_async_copy(down_hbm, down_ref, sems.at[0]),
        pltpu.make_async_copy(up_hbm, up_ref, sems.at[1]),
    ]
    for copy in copies:
        copy.start()
    order = travel_order(1)
    for copy in copies:
        copy.wait()
    parts = []
    for q in range(4):
        parts.append(down_ref[:, q * QH : q * QH + LO])
        parts.append(
            jnp.concatenate(
                [
                    down_ref[:, q * QH + LO : (q + 1) * QH],
                    up_ref[:, q * QF : (q + 1) * QF],
                    jnp.zeros((32, LO - HI), BF),
                ],
                axis=1,
            )
        )
    parts = jnp.concatenate(parts, axis=0)
    for half in range(2):
        rows = slice(half * 128, half * 128 + 128)
        out_ref[rows, :] = dot(order[rows, :], parts).astype(BF)
        rows = pl.ds(half * 128, 128)
        copies.append(
            pltpu.make_async_copy(out_ref.at[rows, :], out_hbm.at[rows, :], sems.at[2 + half])
        )
        copies[-1].start()
    for copy in copies[2:]:
        copy.wait()


def pick_kernel(hits_ref, in_ref, out_ref):
    out_ref[:, :LO] = dot(hits_ref[:512, :], in_ref[...]).astype(BF)
    out_ref[:, LO:] = dot(hits_ref[512:, :], in_ref[:, :HI]).astype(BF)


def quarter(ref, q, lanes):
    tiles = [ref[(rp * 4 + q) * 16 : (rp * 4 + q) * 16 + 16, lanes] for rp in range(8)]
    return jnp.concatenate(tiles, axis=0)


def members(mine_ref):
    k = (iota((128, TOK), 0) >> 1) & 7
    own = k == mine_ref[0:1, :TOK]
    k = (iota((128, EXTRA), 0) >> 1) & 7
    return own, k == mine_ref[0:1, TOK : TOK + EXTRA]


def rank_rows():
    o = iota((RANK, 128), 0)
    i = iota((RANK, 128), 1)
    return (i & 1) * 8 + (i >> 4) == o


def mark_kernel(in_hbm, mine_ref, grad_ref, out_ref):
    out_ref[...] = mine_ref[...]


def score_kernel(grad_ref, in_ref, hid_ref, extra_ref, mine_ref, out_ref):
    quarters = [quarter(in_ref, q, slice(0, ROW)) for q in range(4)]
    tokens = jnp.concatenate([hid_ref[...], extra_ref[:, :HID]], axis=0)
    down = dot(tokens, jnp.concatenate([m[:, :QH] for m in quarters], axis=1), 1, 1)
    tokens = jnp.concatenate([grad_ref[...], extra_ref[:, HID:]], axis=0)
    up = dot(tokens, jnp.concatenate([m[:, QH:] for m in quarters], axis=1), 1, 1)
    mine = mine_ref[:, : TOK + EXTRA].astype(F32).astype(BF)
    mine = dot(mine, jnp.full((8, 128), 0.125, BF), 0, 0)
    member = ((iota((TOK + EXTRA, 128), 1) >> 1) & 7).astype(F32) == mine
    fold = one_hot(rank_rows())
    rows = [dot(fold, jnp.where(member, part, 0.0).astype(BF), 1, 1) for part in (up, down)]
    rows = jnp.concatenate(rows, axis=0)
    block = rows.astype(BF)
    tail = rows[:, TOK:]
    tail = jnp.concatenate([tail[i * 8 : i * 8 + 8, :] for i in range(4)], axis=1).astype(BF)
    for z in range(TP):
        out_ref[z * SIG : z * SIG + 32, :] = block[:, :128]
        out_ref[z * SIG + 32 : z * SIG + 64, :] = block[:, 128:TOK]
        out_ref[z * SIG + 64 : (z + 1) * SIG, :] = tail


def spread_signal(sig_ref, mine_ref, first):
    def total(at, rows):
        part = sig_ref[at : at + rows, :].astype(F32)
        for z in range(1, TP):
            part += sig_ref[z * SIG + at : z * SIG + at + rows, :].astype(F32)
        return part

    tail = total(64, 8)
    at = first * 4
    tail = jnp.concatenate(
        [tail[:, at : at + EXTRA], tail[:, at + EXTRA : at + 2 * EXTRA]], axis=0
    )
    parts = [total(first, RANK), total(32 + first, RANK)]
    own, extra = members(mine_ref)
    fold = one_hot(rank_rows())
    rows = dot(fold, jnp.concatenate(parts, axis=1).astype(BF), 0, 0)
    tail = dot(fold, tail.astype(BF), 0, 0)
    return jnp.where(own, rows, 0.0).astype(BF), jnp.where(extra, tail, 0.0).astype(BF)


def sum_kernel(grad_ref, sig_ref, hid_ref, extra_ref, mine_ref, out_ref):
    up = jnp.concatenate(spread_signal(sig_ref, mine_ref, 0), axis=1)
    down = jnp.concatenate(spread_signal(sig_ref, mine_ref, RANK), axis=1)
    for q in range(4):
        lanes = slice(q * QH, (q + 1) * QH)
        tokens = jnp.concatenate([hid_ref[:, lanes], extra_ref[:, lanes]], axis=0)
        sums = dot(up, tokens)
        for rp in range(8):
            at = (rp * 4 + q) * 16
            out_ref[at : at + 16, :QH] = sums[rp * 16 : rp * 16 + 16, :].astype(BF)
        lanes = slice(q * QF, (q + 1) * QF)
        behind = slice(HID + q * QF, HID + (q + 1) * QF)
        tokens = jnp.concatenate([grad_ref[:, lanes], extra_ref[:, behind]], axis=0)
        sums = dot(down, tokens)
        for rp in range(8):
            at = (rp * 4 + q) * 16
            out_ref[at : at + 16, QH:] = sums[rp * 16 : rp * 16 + 16, :].astype(BF)


def extra_kernel(sig_ref, in_ref, mine_ref, out_ref):
    _, up = spread_signal(sig_ref, mine_ref, 0)
    for q in range(4):
        out_ref[:, q * QH : (q + 1) * QH] = (
            adapter_factor * dot(up, quarter(in_ref, q, slice(0, QH)), 0, 0)
        ).astype(BF)


def hidden_kernel(sig_ref, in_ref, mine_ref, out_hbm, tail_ref, head_ref, sems):
    up, _ = spread_signal(sig_ref, mine_ref, 0)
    cut = TOK - EXTRA
    copies = []
    for q in range(4):
        lanes = slice(q * QH, (q + 1) * QH)
        rows = adapter_factor * dot(up, quarter(in_ref, q, slice(0, QH)), 0, 0)
        head_ref[:, lanes] = rows[:cut, :].astype(BF)
        tail_ref[:, lanes] = rows[cut:, :].astype(BF)
        copies.append(
            pltpu.make_async_copy(
                head_ref.at[:, pl.ds(q * QH, QH)],
                out_hbm.at[pl.ds(0, cut), pl.ds(q * QH, QH)],
                sems.at[q],
            )
        )
        copies[-1].start()
    for copy in copies:
        copy.wait()


def reduce_kernel(hits_ref, in_ref, out_hbm, out_ref, sems):
    def value(lanes):
        sums = dot(hits_ref[:256, :], in_ref[:, lanes])
        if lanes.start < HI:
            sums += dot(hits_ref[256:, :], in_ref[:, LO + lanes.start : LO + lanes.stop])
        return sums

    store_parts(value, out_ref, out_hbm, sems, 0)


def join_kernel(
    head_hbm,
    scale_ref,
    order_ref,
    in_ref,
    tail_ref,
    back_ref,
    hidden_hbm,
    down_hbm,
    up_hbm,
    down_ref,
    up_ref,
    rows_ref,
    sems,
):
    rows_ref[...] = tail_ref[...] + back_ref[...]
    copies = [
        pltpu.make_async_copy(
            rows_ref, hidden_hbm.at[pl.ds(TOK - EXTRA, EXTRA), :], sems.at[8]
        )
    ]
    copies[0].start()
    scale = scale_ref[:, 0:1]
    rows = dot(order_ref[...], in_ref[...])
    for q in range(4):
        low = rows[q * 64 : q * 64 + 32, :] * scale
        high = rows[q * 64 + 32 : q * 64 + 64, :] * scale
        down_ref[:, q * QH : q * QH + LO] = low
        down_ref[:, q * QH + LO : (q + 1) * QH] = high[:, : QH - LO]
        up_ref[:, q * QF : (q + 1) * QF] = high[:, QH - LO : HI]
        lanes = pl.ds(q * QH, QH)
        copies.append(
            pltpu.make_async_copy(down_ref.at[:, lanes], down_hbm.at[:, lanes], sems.at[q])
        )
        lanes = pl.ds(q * QF, QF)
        copies.append(pltpu.make_async_copy(up_ref.at[:, lanes], up_hbm.at[:, lanes], sems.at[4 + q]))
        for copy in copies[-2:]:
            copy.start()
    for copy in copies:
        copy.wait()


def call(kernel, outs, scratch, *args, smem=0, any_in=0, hbm_in=0, hbm_out=0, alias=None, limit=LIMIT):
    vmem = pl.BlockSpec(memory_space=pltpu.VMEM)
    scalar = pl.BlockSpec(memory_space=pltpu.SMEM)
    hbm = pl.BlockSpec(memory_space=pltpu.HBM)
    return pl.pallas_call(
        kernel,
        out_shape=[jax.ShapeDtypeStruct(s, t) for s, t in outs],
        in_specs=[scalar] * smem + [pl.BlockSpec(memory_space=pl.ANY)] * any_in
        + [hbm] * hbm_in
        + [vmem] * (len(args) - smem - any_in - hbm_in),
        out_specs=[hbm] * hbm_out + [vmem] * (len(outs) - hbm_out),
        scratch_shapes=scratch,
        input_output_aliases=alias or {},
        compiler_params=pltpu.CompilerParams(vmem_limit_bytes=limit),
    )(*args)


def exchange(x, axis, parts):
    block = x.reshape(parts, x.shape[0] // parts, x.shape[1])
    return lax.all_to_all(block, axis, 0, 0, tiled=True).reshape(x.shape)


def on_device(output_gradient, hidden, adapter_down, adapter_up, counts, offsets, adapter_slot):
    dp = lax.axis_index("dp").astype(I32).reshape(1)
    onward = [(i, i + 1) for i in range(DP - 1)]
    backward = [(i + 1, i) for i in range(DP - 1)]
    last = jnp.concatenate([hidden[TOK - EXTRA :], output_gradient[TOK - EXTRA :]], axis=1)
    extra = lax.ppermute(last, "dp", onward)
    down = adapter_down.reshape(2 * RANK, HID)
    up = adapter_up.reshape(2 * RANK, FEA)
    (cut,) = call(
        cut_kernel,
        [((256, LO), BF)],
        [
            pltpu.VMEM((32, HID), BF),
            pltpu.VMEM((32, FEA), BF),
            pltpu.VMEM((256, LO), BF),
            pltpu.SemaphoreType.DMA((5,)),
        ],
        down,
        up,
        hbm_in=2,
        hbm_out=1,
        limit=63_400_000,
    )
    pieces = exchange(cut, "dp", DP)
    pick_hits, reduce_hits, order, mine, scale = call(
        tables_kernel,
        [
            ((1024, 256), BF),
            ((512, 512), BF),
            ((256, 256), BF),
            ((8, 384), I32),
            ((32, 128), F32),
        ],
        [],
        dp,
        offsets,
        counts,
        adapter_slot,
        smem=4,
    )
    block = ((512, ROW), BF)
    (picked,) = call(pick_kernel, [block], [], pick_hits, pieces)
    local = exchange(picked, "dp", DP)
    (mine,) = call(mark_kernel, [((8, 384), I32)], [], local, mine, output_gradient, any_in=1)
    tokens = (hidden, extra, mine)
    (partial,) = call(score_kernel, [((TP * SIG, 128), BF)], [], output_gradient, local, *tokens)
    signals = exchange(partial, "tensor", TP)
    (sums,) = call(sum_kernel, [block], [], output_gradient, signals, *tokens)
    gathered = exchange(sums, "dp", DP)
    (extra_gradient,) = call(extra_kernel, [((EXTRA, HID), BF)], [], signals, local, mine)
    back = lax.ppermute(extra_gradient, "dp", backward)
    head, tail = call(
        hidden_kernel,
        [((TOK, HID), BF), ((EXTRA, HID), BF)],
        [pltpu.VMEM((TOK - EXTRA, HID), BF), pltpu.SemaphoreType.DMA((4,))],
        signals,
        local,
        mine,
        hbm_out=1,
    )
    (slot_sums,) = call(
        reduce_kernel,
        [((256, LO), BF)],
        [pltpu.VMEM((256, LO), BF), pltpu.SemaphoreType.DMA((3,))],
        reduce_hits,
        gathered,
        hbm_out=1,
    )
    owned = exchange(slot_sums, "dp", DP)
    hidden_gradient, down_gradient, up_gradient = call(
        join_kernel,
        [((TOK, HID), BF), ((32, HID), F32), ((32, FEA), F32)],
        [
            pltpu.VMEM((32, HID), F32),
            pltpu.VMEM((32, FEA), F32),
            pltpu.VMEM((EXTRA, HID), BF),
            pltpu.SemaphoreType.DMA((9,)),
        ],
        head,
        scale,
        order,
        owned,
        tail,
        back,
        hbm_in=1,
        hbm_out=3,
        alias={0: 0},
    )
    return (
        hidden_gradient,
        down_gradient.reshape(2, RANK, HID),
        up_gradient.reshape(2, RANK, FEA),
    )


def solution(mesh):
    placed = (
        P("dp", "tensor"),
        P("dp", "tensor"),
        P("dp", None, "tensor"),
        P("dp", None, "tensor"),
        P(),
        P(),
        P(),
    )
    return jax.shard_map(
        on_device,
        mesh=mesh,
        in_specs=placed,
        out_specs=(P("dp", "tensor"), P("dp", None, "tensor"), P("dp", None, "tensor")),
        check_vma=False,
    )
```

```python
import jax
import jax.numpy as jnp
from jax import lax
from jax.experimental import pallas as pl
from jax.experimental.pallas import tpu as pltpu
from jax.sharding import PartitionSpec as P


adapter_factor = 2.0
BF = jnp.bfloat16
F32 = jnp.float32
I32 = jnp.int32
DP = 32
TP = 8
SLOTS = 64
RANK = 16
TOK = 256
HID = 3584
FEA = 1024
QH = HID // 4
QF = FEA // 4
ROW = QH + QF
LO = 640
HI = ROW - LO
EXTRA = 32
SIG = 72
LIMIT = 16 * 1024 * 1024


def iota(shape, axis):
    return lax.broadcasted_iota(I32, shape, axis)


def one_hot(condition):
    return jnp.where(condition, 1.0, 0.0).astype(BF)


def dot(a, b, ca=1, cb=0):
    return lax.dot_general(a, b, (((ca,), (cb,)), ((), ())), preferred_element_type=F32)


def travel_order(axis):
    i = iota((256, 256), 1 - axis)
    j = iota((256, 256), axis)
    rp, q, s, r, h = i >> 5, (i >> 3) & 3, (i >> 2) & 1, (i >> 1) & 1, i & 1
    return one_hot(j == q * 64 + h * 32 + s * 16 + rp * 2 + r)


def slot_hits(tab, shape, axis, part):
    c = iota(shape, axis)
    i = iota(shape, 1 - axis)
    hit = ((i >> 2).astype(F32) == tab) & (((i >> 1) & 1) == (c & 1)) & ((i & 1) == part)
    return one_hot(hit)


def tables_kernel(
    dp_ref, off_ref, cnt_ref, slot_ref, pick_ref, reduce_ref, order_ref, mine_ref, scale_ref
):
    dp = dp_ref[0]
    i = iota((8, 512), 1)
    first = (i >> 4) * TOK

    def count_before(a, low):
        return low + jnp.where(off_ref[a] + cnt_ref[a] <= first, 1, 0)

    wanted = lax.fori_loop(0, SLOTS, count_before, jnp.zeros((8, 512), I32), unroll=8)
    wanted += (i >> 1) & 7

    p = iota((8, 384), 1)
    own = p < TOK
    start = (dp - jnp.where(own, 0, 1)) * TOK
    at = start + jnp.where(own, p, p - EXTRA)

    def collect(a, carry):
        tab, mine, c0, c1 = carry
        off = off_ref[a]
        slot = slot_ref[a]
        hit = (wanted == a) & (off < first + TOK)
        tab = jnp.where(hit, slot, tab)
        mine = mine + jnp.where((off > start) & (off <= at), 1, 0)
        c0 = jnp.where(slot == 2 * dp, cnt_ref[a], c0)
        c1 = jnp.where(slot == 2 * dp + 1, cnt_ref[a], c1)
        return tab, mine, c0, c1

    init = (jnp.full((8, 512), -1, I32), jnp.zeros((8, 384), I32), jnp.int32(1), jnp.int32(1))
    tab, mine, c0, c1 = lax.fori_loop(0, SLOTS, collect, init, unroll=8)
    column = dot(tab.astype(F32).astype(BF), jnp.full((8, 256), 0.125, BF), 0, 0)
    row = tab[0:1, :].astype(F32)
    for part in range(2):
        pick_ref[part * 512 : (part + 1) * 512, :] = slot_hits(column, (512, 256), 0, part)
        reduce_ref[part * 256 : (part + 1) * 256, :] = slot_hits(row, (256, 512), 1, part)
    order_ref[...] = travel_order(0)
    extra = (p < TOK + EXTRA) & (mine == 8)
    mine_ref[...] = jnp.where(own, mine, jnp.where(extra, 0, -1))
    rows = iota((32, 128), 0)
    scale_ref[...] = adapter_factor / jnp.where(rows < 16, c0, c1).astype(F32)


def store_parts(value, out_ref, out_hbm, sems, first):
    copies = []
    for n, at in enumerate((0, 256, 512)):
        width = min(256, LO - at)
        out_ref[:, at : at + width] = value(slice(at, at + width)).astype(BF)
        lanes = pl.ds(at, width)
        copies.append(
            pltpu.make_async_copy(out_ref.at[:, lanes], out_hbm.at[:, lanes], sems.at[first + n])
        )
        copies[-1].start()
    for copy in copies:
        copy.wait()


def cut_kernel(down_hbm, up_hbm, out_hbm, down_ref, up_ref, out_ref, sems):
    copies = [
        pltpu.make_async_copy(down_hbm, down_ref, sems.at[0]),
        pltpu.make_async_copy(up_hbm, up_ref, sems.at[1]),
    ]
    for copy in copies:
        copy.start()
    order = travel_order(1)
    for copy in copies:
        copy.wait()
    parts = []
    for q in range(4):
        parts.append(down_ref[:, q * QH : q * QH + LO])
        parts.append(
            jnp.concatenate(
                [
                    down_ref[:, q * QH + LO : (q + 1) * QH],
                    up_ref[:, q * QF : (q + 1) * QF],
                    jnp.zeros((32, LO - HI), BF),
                ],
                axis=1,
            )
        )
    parts = jnp.concatenate(parts, axis=0)
    store_parts(lambda lanes: dot(order, parts[:, lanes]), out_ref, out_hbm, sems, 2)


def pick_kernel(hits_ref, in_ref, out_ref):
    out_ref[:, :LO] = dot(hits_ref[:512, :], in_ref[...]).astype(BF)
    out_ref[:, LO:] = dot(hits_ref[512:, :], in_ref[:, :HI]).astype(BF)


def quarter(ref, q, lanes):
    tiles = [ref[(rp * 4 + q) * 16 : (rp * 4 + q) * 16 + 16, lanes] for rp in range(8)]
    return jnp.concatenate(tiles, axis=0)


def members(mine_ref):
    k = (iota((128, TOK), 0) >> 1) & 7
    own = k == mine_ref[0:1, :TOK]
    k = (iota((128, EXTRA), 0) >> 1) & 7
    return own, k == mine_ref[0:1, TOK : TOK + EXTRA]


def rank_rows():
    o = iota((RANK, 128), 0)
    i = iota((RANK, 128), 1)
    return (i & 1) * 8 + (i >> 4) == o


def mark_kernel(in_hbm, mine_ref, grad_ref, out_ref):
    out_ref[...] = mine_ref[...]


def score_kernel(grad_ref, in_ref, hid_ref, extra_ref, mine_ref, out_ref):
    up = jnp.zeros((TOK + EXTRA, 128), F32)
    down = jnp.zeros((TOK + EXTRA, 128), F32)
    for q in range(4):
        lanes = slice(q * QH, (q + 1) * QH)
        tokens = jnp.concatenate([hid_ref[:, lanes], extra_ref[:, lanes]], axis=0)
        down += dot(tokens, quarter(in_ref, q, slice(0, QH)), 1, 1)
        lanes = slice(q * QF, (q + 1) * QF)
        behind = slice(HID + q * QF, HID + (q + 1) * QF)
        tokens = jnp.concatenate([grad_ref[:, lanes], extra_ref[:, behind]], axis=0)
        up += dot(tokens, quarter(in_ref, q, slice(QH, ROW)), 1, 1)
    mine = mine_ref[:, : TOK + EXTRA].astype(F32).astype(BF)
    mine = dot(mine, jnp.full((8, 128), 0.125, BF), 0, 0)
    member = ((iota((TOK + EXTRA, 128), 1) >> 1) & 7).astype(F32) == mine
    fold = one_hot(rank_rows())
    rows = [dot(fold, jnp.where(member, part, 0.0).astype(BF), 1, 1) for part in (up, down)]
    rows = jnp.concatenate(rows, axis=0)
    block = rows.astype(BF)
    tail = rows[:, TOK:]
    tail = jnp.concatenate([tail[i * 8 : i * 8 + 8, :] for i in range(4)], axis=1).astype(BF)
    for z in range(TP):
        out_ref[z * SIG : z * SIG + 32, :] = block[:, :128]
        out_ref[z * SIG + 32 : z * SIG + 64, :] = block[:, 128:TOK]
        out_ref[z * SIG + 64 : (z + 1) * SIG, :] = tail


def spread_signal(sig_ref, mine_ref, first):
    def total(at, rows):
        part = sig_ref[at : at + rows, :].astype(F32)
        for z in range(1, TP):
            part += sig_ref[z * SIG + at : z * SIG + at + rows, :].astype(F32)
        return part

    tail = total(64, 8)
    at = first * 4
    tail = jnp.concatenate(
        [tail[:, at : at + EXTRA], tail[:, at + EXTRA : at + 2 * EXTRA]], axis=0
    )
    parts = [total(first, RANK), total(32 + first, RANK)]
    own, extra = members(mine_ref)
    fold = one_hot(rank_rows())
    rows = dot(fold, jnp.concatenate(parts, axis=1).astype(BF), 0, 0)
    tail = dot(fold, tail.astype(BF), 0, 0)
    return jnp.where(own, rows, 0.0).astype(BF), jnp.where(extra, tail, 0.0).astype(BF)


def sum_kernel(grad_ref, sig_ref, hid_ref, extra_ref, mine_ref, out_ref):
    up = jnp.concatenate(spread_signal(sig_ref, mine_ref, 0), axis=1)
    down = jnp.concatenate(spread_signal(sig_ref, mine_ref, RANK), axis=1)
    for q in range(4):
        lanes = slice(q * QH, (q + 1) * QH)
        tokens = jnp.concatenate([hid_ref[:, lanes], extra_ref[:, lanes]], axis=0)
        sums = dot(up, tokens)
        for rp in range(8):
            at = (rp * 4 + q) * 16
            out_ref[at : at + 16, :QH] = sums[rp * 16 : rp * 16 + 16, :].astype(BF)
        lanes = slice(q * QF, (q + 1) * QF)
        behind = slice(HID + q * QF, HID + (q + 1) * QF)
        tokens = jnp.concatenate([grad_ref[:, lanes], extra_ref[:, behind]], axis=0)
        sums = dot(down, tokens)
        for rp in range(8):
            at = (rp * 4 + q) * 16
            out_ref[at : at + 16, QH:] = sums[rp * 16 : rp * 16 + 16, :].astype(BF)


def extra_kernel(sig_ref, in_ref, mine_ref, out_ref):
    _, up = spread_signal(sig_ref, mine_ref, 0)
    for q in range(4):
        out_ref[:, q * QH : (q + 1) * QH] = (
            adapter_factor * dot(up, quarter(in_ref, q, slice(0, QH)), 0, 0)
        ).astype(BF)


def hidden_kernel(sig_ref, in_ref, mine_ref, out_hbm, tail_ref, head_ref, sems):
    up, _ = spread_signal(sig_ref, mine_ref, 0)
    cut = TOK - EXTRA
    copies = []
    for q in range(4):
        lanes = slice(q * QH, (q + 1) * QH)
        rows = adapter_factor * dot(up, quarter(in_ref, q, slice(0, QH)), 0, 0)
        head_ref[:, lanes] = rows[:cut, :].astype(BF)
        tail_ref[:, lanes] = rows[cut:, :].astype(BF)
        copies.append(
            pltpu.make_async_copy(
                head_ref.at[:, pl.ds(q * QH, QH)],
                out_hbm.at[pl.ds(0, cut), pl.ds(q * QH, QH)],
                sems.at[q],
            )
        )
        copies[-1].start()
    for copy in copies:
        copy.wait()


def reduce_kernel(hits_ref, in_ref, out_hbm, out_ref, sems):
    def value(lanes):
        sums = dot(hits_ref[:256, :], in_ref[:, lanes])
        if lanes.start < HI:
            sums += dot(hits_ref[256:, :], in_ref[:, LO + lanes.start : LO + lanes.stop])
        return sums

    store_parts(value, out_ref, out_hbm, sems, 0)


def join_kernel(
    head_hbm,
    scale_ref,
    order_ref,
    in_ref,
    tail_ref,
    back_ref,
    hidden_hbm,
    down_hbm,
    up_hbm,
    down_ref,
    up_ref,
    rows_ref,
    sems,
):
    rows_ref[...] = tail_ref[...] + back_ref[...]
    copies = [
        pltpu.make_async_copy(
            rows_ref, hidden_hbm.at[pl.ds(TOK - EXTRA, EXTRA), :], sems.at[8]
        )
    ]
    copies[0].start()
    scale = scale_ref[:, 0:1]
    rows = dot(order_ref[...], in_ref[...])
    for q in range(4):
        low = rows[q * 64 : q * 64 + 32, :] * scale
        high = rows[q * 64 + 32 : q * 64 + 64, :] * scale
        down_ref[:, q * QH : q * QH + LO] = low
        down_ref[:, q * QH + LO : (q + 1) * QH] = high[:, : QH - LO]
        up_ref[:, q * QF : (q + 1) * QF] = high[:, QH - LO : HI]
        lanes = pl.ds(q * QH, QH)
        copies.append(
            pltpu.make_async_copy(down_ref.at[:, lanes], down_hbm.at[:, lanes], sems.at[q])
        )
        lanes = pl.ds(q * QF, QF)
        copies.append(pltpu.make_async_copy(up_ref.at[:, lanes], up_hbm.at[:, lanes], sems.at[4 + q]))
        for copy in copies[-2:]:
            copy.start()
    for copy in copies:
        copy.wait()


def call(kernel, outs, scratch, *args, smem=0, any_in=0, hbm_in=0, hbm_out=0, alias=None, limit=LIMIT):
    vmem = pl.BlockSpec(memory_space=pltpu.VMEM)
    scalar = pl.BlockSpec(memory_space=pltpu.SMEM)
    hbm = pl.BlockSpec(memory_space=pltpu.HBM)
    return pl.pallas_call(
        kernel,
        out_shape=[jax.ShapeDtypeStruct(s, t) for s, t in outs],
        in_specs=[scalar] * smem + [pl.BlockSpec(memory_space=pl.ANY)] * any_in
        + [hbm] * hbm_in
        + [vmem] * (len(args) - smem - any_in - hbm_in),
        out_specs=[hbm] * hbm_out + [vmem] * (len(outs) - hbm_out),
        scratch_shapes=scratch,
        input_output_aliases=alias or {},
        compiler_params=pltpu.CompilerParams(vmem_limit_bytes=limit),
    )(*args)


def exchange(x, axis, parts):
    block = x.reshape(parts, x.shape[0] // parts, x.shape[1])
    return lax.all_to_all(block, axis, 0, 0, tiled=True).reshape(x.shape)


def on_device(output_gradient, hidden, adapter_down, adapter_up, counts, offsets, adapter_slot):
    dp = lax.axis_index("dp").astype(I32).reshape(1)
    onward = [(i, i + 1) for i in range(DP - 1)]
    backward = [(i + 1, i) for i in range(DP - 1)]
    last = jnp.concatenate([hidden[TOK - EXTRA :], output_gradient[TOK - EXTRA :]], axis=1)
    extra = lax.ppermute(last, "dp", onward)
    down = adapter_down.reshape(2 * RANK, HID)
    up = adapter_up.reshape(2 * RANK, FEA)
    (cut,) = call(
        cut_kernel,
        [((256, LO), BF)],
        [
            pltpu.VMEM((32, HID), BF),
            pltpu.VMEM((32, FEA), BF),
            pltpu.VMEM((256, LO), BF),
            pltpu.SemaphoreType.DMA((5,)),
        ],
        down,
        up,
        hbm_in=2,
        hbm_out=1,
        limit=63_400_000,
    )
    pieces = exchange(cut, "dp", DP)
    pick_hits, reduce_hits, order, mine, scale = call(
        tables_kernel,
        [
            ((1024, 256), BF),
            ((512, 512), BF),
            ((256, 256), BF),
            ((8, 384), I32),
            ((32, 128), F32),
        ],
        [],
        dp,
        offsets,
        counts,
        adapter_slot,
        smem=4,
    )
    block = ((512, ROW), BF)
    (picked,) = call(pick_kernel, [block], [], pick_hits, pieces)
    local = exchange(picked, "dp", DP)
    (mine,) = call(mark_kernel, [((8, 384), I32)], [], local, mine, output_gradient, any_in=1)
    tokens = (hidden, extra, mine)
    (partial,) = call(score_kernel, [((TP * SIG, 128), BF)], [], output_gradient, local, *tokens)
    signals = exchange(partial, "tensor", TP)
    (sums,) = call(sum_kernel, [block], [], output_gradient, signals, *tokens)
    gathered = exchange(sums, "dp", DP)
    (extra_gradient,) = call(extra_kernel, [((EXTRA, HID), BF)], [], signals, local, mine)
    back = lax.ppermute(extra_gradient, "dp", backward)
    head, tail = call(
        hidden_kernel,
        [((TOK, HID), BF), ((EXTRA, HID), BF)],
        [pltpu.VMEM((TOK - EXTRA, HID), BF), pltpu.SemaphoreType.DMA((4,))],
        signals,
        local,
        mine,
        hbm_out=1,
    )
    (slot_sums,) = call(
        reduce_kernel,
        [((256, LO), BF)],
        [pltpu.VMEM((256, LO), BF), pltpu.SemaphoreType.DMA((3,))],
        reduce_hits,
        gathered,
        hbm_out=1,
    )
    owned = exchange(slot_sums, "dp", DP)
    hidden_gradient, down_gradient, up_gradient = call(
        join_kernel,
        [((TOK, HID), BF), ((32, HID), F32), ((32, FEA), F32)],
        [
            pltpu.VMEM((32, HID), F32),
            pltpu.VMEM((32, FEA), F32),
            pltpu.VMEM((EXTRA, HID), BF),
            pltpu.SemaphoreType.DMA((9,)),
        ],
        head,
        scale,
        order,
        owned,
        tail,
        back,
        hbm_in=1,
        hbm_out=3,
        alias={0: 0},
    )
    return (
        hidden_gradient,
        down_gradient.reshape(2, RANK, HID),
        up_gradient.reshape(2, RANK, FEA),
    )


def solution(mesh):
    placed = (
        P("dp", "tensor"),
        P("dp", "tensor"),
        P("dp", None, "tensor"),
        P("dp", None, "tensor"),
        P(),
        P(),
        P(),
    )
    return jax.shard_map(
        on_device,
        mesh=mesh,
        in_specs=placed,
        out_specs=(P("dp", "tensor"), P("dp", None, "tensor"), P("dp", None, "tensor")),
        check_vma=False,
    )
```
